256 devices in a mesh: seq: 32 (over y, x, core), head: 8 (over z).
Axes of the slice: x: 4, y: 4, z: 8, core: 2. Of those that a mesh axis runs over, the one named last changes fastest.
Arguments:
- queries: bfloat16 [32768, 32, 128], P('seq', 'head'), may hold values from -6 to 6
- keys: bfloat16 [32768, 32, 128], P('seq', 'head'), may hold values from -6 to 6
- values: bfloat16 [32768, 32, 128], P('seq', 'head'), may hold values from -6 to 6
- out_grad: bfloat16 [32768, 32, 128], P('seq', 'head'), may hold values from -6 to 6
- level_codes: int32 [21, 32768], P(None, ('seq', 'head')), may hold values from 1 to 16
Outputs:
- query_grad: bfloat16 [32768, 32, 128], P('seq', 'head')
- key_grad: bfloat16 [32768, 32, 128], P('seq', 'head')
- value_grad: bfloat16 [32768, 32, 128], P('seq', 'head')
The draws below stay inside these ranges and needn't reach their ends.
Inputs may be any that keep to these rules, and one draw needn't show every extreme that they name: `level_codes`: level codes are whole numbers.
All inputs are finite; a program needn't handle non-finite values.
Results may differ from the reference program's by a relative error of at most 0.0052.
Values sent between devices are 32-bit elements; how exact they have to be, the bound alone decides.
A program may use at most 128 MiB of HBM per device.

```python
import jax
import jax.numpy as jnp
from jax import lax

H = 32
HD = 128
LEVELS = 21
TOK_DEV = 1024
TOKENS = 32768


def set_ends(array, key, least, largest):
    shape = array.shape
    spot = [jax.random.randint(jax.random.fold_in(key, axis), (), 0, shape[axis]) for axis in range(len(shape))]
    array = array.at[tuple(spot)].set(least)
    longest = shape.index(max(shape))
    spot[longest] = (spot[longest] + 1) % shape[longest]
    return array.at[tuple(spot)].set(largest)


def levels(stream_key, extent, pieces, low, largest):
    def one(position, shards_of):
        steps = jax.random.uniform(jax.random.fold_in(jax.random.fold_in(stream_key, 6), position), (shards_of,), jnp.float32, low / len(pieces), largest / len(pieces))
        return jnp.repeat(jnp.exp(steps), extent[position] // shards_of).reshape((-1,) + (1,) * (len(extent) - position - 1))

    loudness = one(*pieces[0])
    for cut in pieces[1:]:
        loudness = loudness * one(*cut)
    return loudness


def noise(rng, extent, scale, most, cuts=(), kind=jnp.bfloat16):
    entries = scale * jax.random.normal(rng, extent, jnp.float32)
    if cuts:
        entries = entries * levels(rng, extent, cuts, -0.22, 0.18)
    return jnp.clip(entries, -most, most).astype(kind)


def setup_inputs(seed: int = 0) -> dict:
    arg_keys = jax.random.split(jax.random.key(seed), 6)
    return {
        "queries": noise(arg_keys[0], (TOKENS, H, HD), 1.0, 6.0, ((0, 32), (1, 8))),
        "keys": noise(arg_keys[1], (TOKENS, H, HD), 1.0, 6.0, ((0, 32), (1, 8))),
        "values": noise(arg_keys[2], (TOKENS, H, HD), 1.0, 6.0, ((0, 32), (1, 8))),
        "out_grad": noise(arg_keys[3], (TOKENS, H, HD), 1.0, 6.0, ((0, 32), (1, 8))),
        "level_codes": set_ends(jax.random.randint(arg_keys[4], (LEVELS, TOKENS), 1, 17), jax.random.fold_in(arg_keys[4], 1), 1, 16).astype(jnp.int32),
    }


def level_weights(codes):
    order = jnp.arange(codes.shape[0], dtype=jnp.float32)
    factor = jnp.exp2(-0.5 * jnp.maximum(order - 1.0, 0.0)) / 16.0
    return codes.astype(jnp.float32) * factor[:, None]


def level_matrix(count, bits):
    rows = jnp.arange(count, dtype=jnp.int32)[:, None]
    cols = jnp.arange(count, dtype=jnp.int32)[None, :]
    differ = jnp.bitwise_xor(rows, cols)
    depth = jnp.zeros((count, count), jnp.int32)
    for power in range(bits):
        depth = depth + (differ >= (1 << power)).astype(jnp.int32)
    return jnp.where(cols <= rows, depth, -1)


def level_mask(depth, lam, bits):
    mask = jnp.zeros(depth.shape, jnp.float32)
    for level in range(bits + 1):
        mask = mask + jnp.where(depth == level, lam[level][:, None], 0.0)
    return mask


def local_head(mask, scale, query, key, value, grad):
    inner = (((1,), (1,)), ((), ()))
    outer = (((0,), (0,)), ((), ()))
    scores = lax.dot_general(query, key, inner, preferred_element_type=jnp.float32)
    dprob = lax.dot_general(grad, value, inner, preferred_element_type=jnp.float32)
    weight_q = (mask * (scale * dprob)).astype(jnp.bfloat16)
    weight_v = (mask * (scale * scores)).astype(jnp.bfloat16)
    dquery = jnp.dot(weight_q, key, preferred_element_type=jnp.float32)
    dkey = lax.dot_general(weight_q, query, outer, preferred_element_type=jnp.float32)
    dvalue = lax.dot_general(weight_v, grad, outer, preferred_element_type=jnp.float32)
    return dquery, dkey, dvalue


def reference(queries, keys, values, out_grad, level_codes):
    tokens, heads, width = queries.shape
    scale = width ** -0.5
    groups = tokens // TOK_DEV
    local_bits = TOK_DEV.bit_length() - 1
    tree_bits = groups.bit_length() - 1
    highest = lax.Precision.HIGHEST
    lam = level_weights(level_codes)
    lam_blocks = jnp.swapaxes(lam.reshape(lam.shape[0], groups, TOK_DEV), 0, 1)
    depth = level_matrix(TOK_DEV, local_bits)
    owners = jnp.arange(groups, dtype=jnp.int32)
    bit_rows = [jnp.bitwise_and(jnp.right_shift(owners, b), 1) for b in range(tree_bits)]
    on_bits = jnp.stack(bit_rows, axis=1).astype(jnp.float32)
    partner_rows = [(jnp.right_shift(owners[None, :], b) == jnp.bitwise_xor(jnp.right_shift(owners[:, None], b), 1)) for b in range(tree_bits)]
    picks = jnp.stack(partner_rows, axis=1).astype(jnp.float32)
    select = picks * on_bits[:, :, None]
    lam_cross = lam_blocks[:, local_bits + 1: local_bits + 1 + tree_bits] * on_bits[:, :, None]

    def one_head(items):
        query, key, value, grad = items
        query_blocks = query.reshape(groups, TOK_DEV, width)
        key_blocks = key.reshape(groups, TOK_DEV, width)
        value_blocks = value.reshape(groups, TOK_DEV, width)
        grad_blocks = grad.reshape(groups, TOK_DEV, width)

        def one_block(block):
            block_q, block_k, block_v, block_g, block_lam = block
            mask = level_mask(depth, block_lam, local_bits)
            return local_head(mask, scale, block_q, block_k, block_v, block_g)

        local_q, local_k, local_v = lax.map(one_block, (query_blocks, key_blocks, value_blocks, grad_blocks, lam_blocks))
        query32 = query_blocks.astype(jnp.float32)
        key32 = key_blocks.astype(jnp.float32)
        value32 = value_blocks.astype(jnp.float32)
        grad32 = grad_blocks.astype(jnp.float32)
        state = jnp.einsum("ntx,nty->nxy", key32, value32, precision=highest)
        cross = jnp.einsum("jbi,ixy->jbxy", select, state, precision=highest)
        cross_half = cross.astype(jnp.bfloat16).astype(jnp.float32)
        projected = jnp.einsum("jty,jbxy->jbtx", grad32, cross_half, precision=highest)
        cross_q = scale * jnp.einsum("jbt,jbtx->jtx", lam_cross, projected, precision=highest)
        weighted = (lam_cross[:, :, :, None] * query32[:, None]).astype(jnp.bfloat16).astype(jnp.float32)
        level_grad = scale * jnp.einsum("jbtx,jty->jbxy", weighted, grad32, precision=highest)
        key_state = jnp.einsum("jbi,jbxy->ixy", select, level_grad, precision=highest)
        key_half = key_state.astype(jnp.bfloat16).astype(jnp.float32)
        cross_k = jnp.einsum("ixy,ity->itx", key_half, value32, precision=highest)
        cross_v = jnp.einsum("ixy,itx->ity", key_half, key32, precision=highest)
        dquery = (local_q + cross_q).reshape(tokens, width).astype(jnp.bfloat16)
        dkey = (local_k + cross_k).reshape(tokens, width).astype(jnp.bfloat16)
        dvalue = (local_v + cross_v).reshape(tokens, width).astype(jnp.bfloat16)
        return dquery, dkey, dvalue

    heads_first = (jnp.swapaxes(queries, 0, 1), jnp.swapaxes(keys, 0, 1), jnp.swapaxes(values, 0, 1), jnp.swapaxes(out_grad, 0, 1))
    dquery, dkey, dvalue = lax.map(one_head, heads_first)
    return (jnp.swapaxes(dquery, 0, 1), jnp.swapaxes(dkey, 0, 1), jnp.swapaxes(dvalue, 0, 1))
```

```python
import functools

import jax
import jax.numpy as jnp
from jax import lax
from jax.experimental import pallas as pl
from jax.experimental.pallas import tpu as pltpu
from jax.sharding import PartitionSpec as P

MESH = pl.DeviceIdType.MESH
F32 = jnp.float32
BF16 = jnp.bfloat16
CHUNK = 128
INNER = 3
CROSS = 5
ROWS = 16
PARTNERS = (1, 2, 6, 8, 24)

NN = (((1,), (0,)), ((), ()))
NT = (((1,), (1,)), ((), ()))
TN = (((0,), (0,)), ((), ()))


def dot(a, b, dims=NN):
    return lax.dot_general(a, b, dims, preferred_element_type=F32)


def factor(level):
    return 2.0 ** (-0.5 * max(level - 1, 0)) / 16.0


def on_bit(index, bit):
    return lax.rem(jnp.right_shift(index, bit), 2).astype(F32)


def spread(codes, first, count):
    rows = lax.broadcasted_iota(jnp.int32, (codes.shape[0], count * CHUNK), 0)
    cols = lax.broadcasted_iota(jnp.int32, (codes.shape[0], count * CHUNK), 1)
    pick = (rows == first + jnp.right_shift(cols, 7)).astype(F32).astype(BF16)
    return dot(codes.astype(F32).astype(BF16), pick, TN)


def split_heads(flat, tmp, out):
    heads, count, _ = out.shape
    tmp[...] = flat[...].astype(F32)
    for h in range(heads):
        out[h] = tmp[pl.ds(h, count, stride=heads), :].astype(BF16)


def exchange_kernel(
    scale, zs,
    q_in, k_in, v_in, g_in, codes_in,
    qh_out, kh_out, vh_out, gh_out, codes_out, cross_out, ks_out,
    flat, tmp, qh, kh, vh, gh, lam, weighted,
    state, r_state, tot, r_tot, r_found,
    level, r_level, r_level0, down, r_down, mid, r_mid,
    in_sem, out_sem, code_send, code_recv, send, recv,
):
    seq = lax.axis_index("seq")
    z = lax.axis_index("head")
    mine = 2 * lax.rem(seq, 2)
    theirs = 2 - mine
    heads, count, _ = qh.shape
    partner = [jnp.bitwise_xor(seq, p) for p in PARTNERS]

    barrier = pltpu.get_barrier_semaphore()
    for p in partner:
        pl.semaphore_signal(barrier, inc=1, device_id=(p, z), device_id_type=MESH)
    for d in range(1, zs):
        pl.semaphore_signal(
            barrier, inc=1, device_id=(seq, lax.rem(z + d, zs)), device_id_type=MESH)

    loads = [
        pltpu.make_async_copy(src, flat.at[i], in_sem.at[i])
        for i, src in enumerate((k_in, v_in, q_in, g_in))
    ]
    for c in loads:
        c.start()

    sent = []

    def remote(src, dst, to):
        n = len(sent)
        c = pltpu.make_async_remote_copy(
            src_ref=src, dst_ref=dst, send_sem=send.at[n], recv_sem=recv.at[n],
            device_id=(partner[to], z), device_id_type=MESH)
        sent.append(c)
        c.start()
        return c

    outs = []

    def put(i, src, dst):
        c = pltpu.make_async_copy(src, dst, out_sem.at[i])
        c.start()
        outs.append(c)

    loads[0].wait()
    split_heads(flat.at[0], tmp, kh)
    put(0, kh, kh_out)
    loads[1].wait()
    split_heads(flat.at[1], tmp, vh)
    put(1, vh, vh_out)
    for h in range(heads):
        state[h] = dot(vh[h], kh[h], TN)

    pl.semaphore_wait(barrier, len(partner) + zs - 1)
    codes_sent = []
    for d in range(1, zs):
        c = pltpu.make_async_remote_copy(
            src_ref=codes_in, dst_ref=codes_out.at[z], send_sem=code_send.at[d - 1],
            recv_sem=code_recv.at[d - 1], device_id=(seq, lax.rem(z + d, zs)),
            device_id_type=MESH)
        c.start()
        codes_sent.append(c)
    s_their = remote(state.at[pl.ds(theirs, 2)], r_state.at[pl.ds(theirs, 2)], 0)
    s_mine = remote(state.at[pl.ds(mine, 2)], r_state.at[pl.ds(mine, 2)], 0)
    codes_out[z] = codes_in[...]

    loads[2].wait()
    split_heads(flat.at[2], tmp, qh)
    put(2, qh, qh_out)

    s_their.wait_recv()
    up = []
    now = []
    for i in range(2):
        tot[0, i] = state[mine + i] + r_state[mine + i]
        now.append(remote(tot.at[0, i], r_tot.at[0, i], 1))
    up.append(now)

    loads[3].wait()
    split_heads(flat.at[3], tmp, gh)
    put(3, gh, gh_out)

    def step_up(p):
        now = []
        for i in range(2):
            up[p - 1][i].wait_recv()
            tot[p, i] = tot[p - 1, i] + r_tot[p - 1, i]
            now.append(remote(tot.at[p, i], r_tot.at[p, i], p + 1))
        up.append(now)

    for c in codes_sent:
        c.wait_recv()

    @pl.loop(0, zs)
    def _(c):
        wide = spread(codes_out[c], 11, CROSS)
        for b in range(CROSS):
            cols = pl.ds(b * CHUNK, CHUNK)
            lam[pl.ds(c * CHUNK, CHUNK), cols] = wide[:, b * CHUNK : (b + 1) * CHUNK] * (
                factor(11 + b) * on_bit(seq, b))

    step_up(1)

    @pl.loop(0, heads)
    def _(h):
        query = qh[h].astype(F32)
        for b in range(CROSS):
            cols = pl.ds(b * CHUNK, CHUNK)
            weighted[:, cols] = (lam[:, cols] * query).astype(BF16)
        result = dot(gh[h], weighted[...], TN)
        for b in range(CROSS):
            level[b, h] = scale * result[:, b * CHUNK : (b + 1) * CHUNK]

    halves = [None] * CROSS
    for b in (4, 3, 2, 1):
        halves[b] = remote(
            level.at[b, pl.ds(theirs, 2)], r_level.at[b - 1, pl.ds(theirs, 2)], 0)
    whole = remote(level.at[0], r_level0, 0)

    step_up(2)
    halves[4].wait_recv()
    down_now = []
    for i in range(2):
        down[0, i] = level[4, mine + i] + r_level[3, mine + i]
        down_now.append(remote(down.at[0, i], r_down.at[0, i], 4))
    step_up(3)
    for n, b in enumerate((3, 2, 1)):
        halves[b].wait_recv()
        after = []
        for i in range(2):
            down_now[i].wait_recv()
            if n == 0:
                mid[n, i] = r_down[n, i]
            else:
                mid[n, i] = mid[n - 1, i] + r_down[n, i]
            down[n + 1, i] = mid[n, i] + level[b, mine + i] + r_level[b - 1, mine + i]
            after.append(remote(down.at[n + 1, i], r_down.at[n + 1, i], b))
        down_now = after
        if n == 1:
            found = []
            for p in range(4):
                for i in range(2):
                    if p == 3:
                        up[p][i].wait_recv()
                    found.append(remote(r_tot.at[p, i], r_found.at[p, i], 0))
    last = []
    for i in range(2):
        down_now[i].wait_recv()
        mid[3, i] = mid[2, i] + r_down[3, i]
        last.append(remote(mid.at[3, i], r_mid.at[i], 0))

    s_mine.wait_recv()
    for h in range(heads):
        cross_out[0, h] = r_state[h].astype(BF16)
    for p in range(4):
        for i in range(2):
            found[2 * p + i].wait_recv()
            cross_out[p + 1, mine + i] = r_tot[p, i].astype(BF16)
            cross_out[p + 1, theirs + i] = r_found[p, i].astype(BF16)
    whole.wait_recv()
    for i in range(2):
        ks_out[mine + i] = mid[3, i] + r_level0[mine + i]
    for i in range(2):
        last[i].wait_recv()
        ks_out[theirs + i] = r_mid[i] + r_level0[theirs + i]

    for c in sent + codes_sent:
        c.wait_send()
    for c in outs:
        c.wait()


def exchange(scale, zs, q, k, v, g, codes):
    heads, count, width = 4, q.shape[0] // 4, q.shape[1]
    square = (width, width)
    any_space = pl.BlockSpec(memory_space=pl.ANY)
    vmem = pl.BlockSpec(memory_space=pltpu.VMEM)
    split = jax.ShapeDtypeStruct((heads, count, width), BF16)
    messages = 2 + 8 + 8 + 4 + 1 + 8 + 2
    return pl.pallas_call(
        functools.partial(exchange_kernel, scale, zs),
        out_shape=(
            split, split, split, split,
            jax.ShapeDtypeStruct((zs, ROWS, CHUNK), jnp.int32),
            jax.ShapeDtypeStruct((CROSS, heads, *square), BF16),
            jax.ShapeDtypeStruct((heads, *square), F32),
        ),
        in_specs=[any_space] * 4 + [vmem],
        out_specs=(any_space,) * 4 + (vmem,) * 3,
        scratch_shapes=[
            pltpu.VMEM((4, heads * count, width), BF16),
            pltpu.VMEM((heads * count, width), F32),
            *[pltpu.VMEM((heads, count, width), BF16)] * 4,
            pltpu.VMEM((count, CROSS * width), F32),
            pltpu.VMEM((count, CROSS * width), BF16),
            pltpu.VMEM((heads, *square), F32),
            pltpu.VMEM((heads, *square), F32),
            *[pltpu.VMEM((4, 2, *square), F32)] * 3,
            pltpu.VMEM((CROSS, heads, *square), F32),
            pltpu.VMEM((4, heads, *square), F32),
            pltpu.VMEM((heads, *square), F32),
            *[pltpu.VMEM((4, 2, *square), F32)] * 3,
            pltpu.VMEM((2, *square), F32),
            pltpu.SemaphoreType.DMA((4,)),
            pltpu.SemaphoreType.DMA((4,)),
            pltpu.SemaphoreType.DMA((zs - 1,)),
            pltpu.SemaphoreType.DMA((zs - 1,)),
            pltpu.SemaphoreType.DMA((messages,)),
            pltpu.SemaphoreType.DMA((messages,)),
        ],
        compiler_params=pltpu.CompilerParams(
            collective_id=0, has_side_effects=True, vmem_limit_bytes=60 << 20),
        name="exchange",
    )(q, k, v, g, codes)


def local_kernel(
    scale,
    seq_ref, qh, kh, vh, gh, codes, cross, ks,
    dq_out, dk_out, dv_out,
    states, sums, mask, out_q, out_k, out_v,
):
    c = pl.program_id(0)
    heads, count, width = qh.shape
    chunks = count // CHUNK

    @pl.when(c == 0)
    def _():
        lam = []
        for n in range(chunks):
            wide = spread(codes[n], 8, INNER)
            lam.append([
                wide[:, b * CHUNK : (b + 1) * CHUNK] * factor(8 + b) for b in range(INNER)])

        @pl.loop(0, heads)
        def _(h):
            one = []
            grads = {}
            for n in range(chunks):
                rows = pl.ds(n * CHUNK, CHUNK)
                one.append(dot(vh[h, rows], kh[h, rows], TN))
                bits = [b for b in range(INNER) if n >> b & 1]
                if bits:
                    query = qh[h, rows].astype(F32)
                    wide = jnp.concatenate(
                        [(lam[n][b] * query).astype(BF16) for b in bits], axis=1)
                    res = dot(gh[h, rows], wide, TN)
                    for m, b in enumerate(bits):
                        grads[n, b] = scale * res[:, m * CHUNK : (m + 1) * CHUNK]
            base = ks[h]
            for n in range(chunks):
                total = base
                for b in range(INNER):
                    group = [i for i in range(chunks) if i >> b == (n >> b) ^ 1]
                    if n >> b & 1:
                        acc = one[group[0]]
                        for i in group[1:]:
                            acc = acc + one[i]
                        states[n, b, h] = acc.astype(BF16)
                    else:
                        acc = grads[group[0], b]
                        for i in group[1:]:
                            acc = acc + grads[i, b]
                        total = total + acc
                sums[n, h] = total.astype(BF16)

    seq = seq_ref[0]
    rows = pl.ds(c * CHUNK, CHUNK)
    here = codes[c]
    lines = [here[n : n + 1, :].astype(F32) * (factor(n) * scale) for n in range(INNER + 5)]
    s_at = lax.broadcasted_iota(jnp.int32, (CHUNK, CHUNK), 0)
    t_at = lax.broadcasted_iota(jnp.int32, (CHUNK, CHUNK), 1)
    differ = jnp.bitwise_xor(s_at, t_at)
    full = jnp.broadcast_to(lines[0], (CHUNK, CHUNK))
    for n in range(7):
        full = jnp.where(differ >= 1 << n, lines[n + 1], full)
    mask[...] = jnp.where(s_at <= t_at, full, 0.0)

    wide = spread(here, 8, INNER + CROSS)
    lam = []
    for b in range(INNER):
        on = lax.rem(jnp.right_shift(c, b), 2).astype(F32)
        lam.append(wide[:, b * CHUNK : (b + 1) * CHUNK] * (factor(8 + b) * scale * on))
    for b in range(CROSS):
        at = INNER + b
        lam.append(wide[:, at * CHUNK : (at + 1) * CHUNK]
                   * (factor(11 + b) * scale * on_bit(seq, b)))

    @pl.when(c == 0)
    def _():
        for n in range(chunks):
            for b in range(INNER):
                if not n >> b & 1:
                    states[n, b] = jnp.zeros(states.shape[2:], BF16)

    for h in range(heads):
        query, key, value, grad = qh[h, rows], kh[h, rows], vh[h, rows], gh[h, rows]
        weight_q = (mask[...] * dot(value, grad, NT)).astype(BF16)
        weight_v = (mask[...] * dot(key, query, NT)).astype(BF16)
        above = sums[c, h]
        dk = dot(weight_q, query) + dot(value, above)
        dv = dot(weight_v, grad) + dot(key, above, NT)
        grad32 = grad.astype(F32)
        dq = dot(weight_q, key, TN)
        for b in range(INNER):
            dq = dq + dot((lam[b] * grad32).astype(BF16), states[c, b, h])
        for b in range(CROSS):
            dq = dq + dot((lam[INNER + b] * grad32).astype(BF16), cross[b, h])
        at = pl.ds(h, CHUNK, stride=heads)
        out_q[at, :] = dq
        out_k[at, :] = dk
        out_v[at, :] = dv
    dq_out[...] = out_q[...].astype(BF16)
    dk_out[...] = out_k[...].astype(BF16)
    dv_out[...] = out_v[...].astype(BF16)


def local(scale, seq, qh, kh, vh, gh, codes, cross, ks):
    heads, count, width = qh.shape
    chunks = count // CHUNK
    vmem = pl.BlockSpec(memory_space=pltpu.VMEM)
    flat = jax.ShapeDtypeStruct((heads * count, width), BF16)
    return pl.pallas_call(
        functools.partial(local_kernel, scale),
        grid=(chunks,),
        out_shape=(flat, flat, flat),
        in_specs=[pl.BlockSpec(memory_space=pltpu.SMEM)] + [vmem] * 7,
        out_specs=(pl.BlockSpec((heads * CHUNK, width), lambda c: (c, 0)),) * 3,
        scratch_shapes=[
            pltpu.VMEM((chunks, INNER, heads, width, width), BF16),
            pltpu.VMEM((chunks, heads, width, width), BF16),
            pltpu.VMEM((CHUNK, CHUNK), F32),
            *[pltpu.VMEM((heads * CHUNK, width), F32)] * 3,
        ],
        compiler_params=pltpu.CompilerParams(vmem_limit_bytes=60 << 20),
        name="local",
    )(seq, qh, kh, vh, gh, codes, cross, ks)


def on_device(queries, keys, values, out_grad, level_codes):
    count, heads, width = queries.shape
    scale = width ** (-0.5)
    flat = [x.reshape(count * heads, width) for x in (queries, keys, values, out_grad)]
    qh, kh, vh, gh, codes, cross, ks = exchange(
        scale, lax.axis_size("head"), *flat, level_codes[:ROWS])
    seq = lax.axis_index("seq").astype(jnp.int32).reshape(1)
    grads = local(scale, seq, qh, kh, vh, gh, codes, cross, ks)
    return tuple(x.reshape(count, heads, width) for x in grads)


def solution(mesh):
    return jax.shard_map(
        on_device,
        mesh=mesh,
        in_specs=(
            P("seq", "head", None),
            P("seq", "head", None),
            P("seq", "head", None),
            P("seq", "head", None),
            P(None, ("seq", "head")),
        ),
        out_specs=(P("seq", "head", None), P("seq", "head", None), P("seq", "head", None)),
        check_vma=False,
    )
```

```python
import functools

import jax
import jax.numpy as jnp
from jax import lax
from jax.experimental import pallas as pl
from jax.experimental.pallas import tpu as pltpu
from jax.sharding import PartitionSpec as P

MESH = pl.DeviceIdType.MESH
F32 = jnp.float32
BF16 = jnp.bfloat16
CHUNK = 128
INNER = 3
CROSS = 5
ROWS = 16
PARTNERS = (1, 2, 6, 8, 24)

NN = (((1,), (0,)), ((), ()))
NT = (((1,), (1,)), ((), ()))
TN = (((0,), (0,)), ((), ()))


def dot(a, b, dims=NN):
    return lax.dot_general(a, b, dims, preferred_element_type=F32)


def factor(level):
    return 2.0 ** (-0.5 * max(level - 1, 0)) / 16.0


def on_bit(index, bit):
    return lax.rem(jnp.right_shift(index, bit), 2).astype(F32)


def spread(codes, first, count):
    rows = lax.broadcasted_iota(jnp.int32, (codes.shape[0], count * CHUNK), 0)
    cols = lax.broadcasted_iota(jnp.int32, (codes.shape[0], count * CHUNK), 1)
    pick = (rows == first + jnp.right_shift(cols, 7)).astype(F32).astype(BF16)
    return dot(codes.astype(F32).astype(BF16), pick, TN)


def split_heads(flat, tmp, out):
    heads, count, _ = out.shape
    tmp[...] = flat[...].astype(F32)
    for h in range(heads):
        out[h] = tmp[pl.ds(h, count, stride=heads), :].astype(BF16)


def chunk(n, count=1):
    return pl.ds(n * CHUNK, count * CHUNK)


PAIRS = (
    (0, (0, 1), (1, 2)), (0, (2, 3), (3, 4)), (0, (4, 5), (5, 6)), (0, (6, 7), (7, 8)),
    (1, (0, 2), (2, 4)), (1, (4, 6), (6, 8)),
    (2, (0, 4), (4, 8)),
)


def exchange_kernel(
    scale, zs,
    q_in, k_in, v_in, g_in, codes_in,
    dq_out, dk_out, dv_out, ks_out, inner_out,
    flat, tmp, qh, kh, vh, gh, gt, lam, codes,
    one, states, inner, mask, dq, flat_k, flat_v, cross,
    state, r_state, tot, r_tot, r_found,
    level, r_level, r_level0, down, r_down, mid, r_mid,
    in_sem, out_sem, code_send, code_recv, send, recv,
):
    seq = lax.axis_index("seq")
    z = lax.axis_index("head")
    mine = 2 * lax.rem(seq, 2)
    theirs = 2 - mine
    heads, count, width = qh.shape
    chunks = count // CHUNK
    subs = range(4)
    half = CHUNK // 2
    partner = [jnp.bitwise_xor(seq, p) for p in PARTNERS]

    barrier = pltpu.get_barrier_semaphore()
    for d in range(1, zs):
        pl.semaphore_signal(
            barrier, inc=1, device_id=(seq, lax.rem(z + d, zs)), device_id_type=MESH)
    for p in partner:
        pl.semaphore_signal(barrier, inc=1, device_id=(p, z), device_id_type=MESH)

    loads = [
        pltpu.make_async_copy(src, flat.at[i], in_sem.at[i])
        for i, src in enumerate((k_in, v_in, q_in, g_in))
    ]
    here = pltpu.make_async_copy(codes_in.at[pl.ds(0, ROWS)], codes.at[z], in_sem.at[4])
    for c in loads:
        c.start()
    here.start()

    sent = []

    def remote(src, dst, to):
        n = len(sent)
        c = pltpu.make_async_remote_copy(
            src_ref=src, dst_ref=dst, send_sem=send.at[n], recv_sem=recv.at[n],
            device_id=(partner[to], z), device_id_type=MESH)
        sent.append(c)
        c.start()
        return c

    outs = []

    def put(src, dst):
        c = pltpu.make_async_copy(src, dst, out_sem.at[len(outs)])
        c.start()
        outs.append(c)

    loads[0].wait()
    split_heads(flat.at[0], tmp, kh)
    loads[1].wait()
    split_heads(flat.at[1], tmp, vh)
    here.wait()

    @pl.loop(0, heads)
    def _(h):
        for n in range(chunks):
            one[n] = dot(vh[h, chunk(n)], kh[h, chunk(n)], TN)
        total = one[0]
        for n in range(1, chunks):
            total = total + one[n]
        state[h] = total
        for m, (_, (lo, hi), _) in enumerate(PAIRS):
            acc = one[lo]
            for n in range(lo + 1, hi):
                acc = acc + one[n]
            states[m, h] = acc.astype(BF16)

    pl.semaphore_wait(barrier, len(partner) + zs - 1)
    codes_sent = []
    for d in range(1, zs):
        c = pltpu.make_async_remote_copy(
            src_ref=codes_in.at[pl.ds(0, ROWS)], dst_ref=codes.at[z],
            send_sem=code_send.at[d - 1], recv_sem=code_recv.at[d - 1],
            device_id=(seq, lax.rem(z + d, zs)), device_id_type=MESH)
        c.start()
        codes_sent.append(c)
    s_their = remote(state.at[pl.ds(theirs, 2)], r_state.at[pl.ds(theirs, 2)], 0)
    s_mine = remote(state.at[pl.ds(mine, 2)], r_state.at[pl.ds(mine, 2)], 0)

    def part(ref, s, *lead):
        return ref[(*lead, mine + s // 2, pl.ds(s % 2 * half, half))]

    loads[2].wait()
    split_heads(flat.at[2], tmp, qh)

    s_their.wait_recv()
    up = [[]]
    for s in subs:
        tot[0, s] = part(state, s) + part(r_state, s)
        up[0].append(remote(tot.at[0, s], r_tot.at[0, s], 1))

    loads[3].wait()
    split_heads(flat.at[3], tmp, gh)

    @pl.loop(0, heads)
    def _(h):
        for n in range(chunks):
            gt[h, :, chunk(n)] = gh[h, chunk(n)].T

    def step_up(p):
        up.append([])
        for s in subs:
            up[p - 1][s].wait_recv()
            tot[p, s] = tot[p - 1, s] + r_tot[p - 1, s]
            up[p].append(remote(tot.at[p, s], r_tot.at[p, s], p + 1))

    def weights(first, number):
        @pl.loop(0, zs)
        def _(c):
            wide = spread(codes[c], 8 + first, number)
            for b in range(number):
                at = first + b
                value = factor(8 + at)
                if at >= INNER:
                    value = value * on_bit(seq, at - INNER)
                lam[chunk(c), chunk(at)] = wide[:, b * CHUNK : (b + 1) * CHUNK] * value

    def level_grad(b, first):
        @pl.loop(0, 2)
        def _(i):
            h = first + i
            wide = (lam[:, chunk(INNER + b)] * qh[h].astype(F32)).astype(BF16)
            level[b, h] = scale * dot(gt[h], wide)

    halves = [None] * CROSS

    def both_grads(b):
        level_grad(b, theirs)
        halves[b] = remote(
            level.at[b, pl.ds(theirs, 2)], r_level.at[b - 1, pl.ds(theirs, 2)], 0)
        level_grad(b, mine)

    for c in codes_sent:
        c.wait_recv()
    weights(INNER + 4, 1)
    both_grads(4)
    step_up(1)
    weights(INNER, 4)
    level_grad(3, theirs)
    halves[3] = remote(level.at[3, pl.ds(theirs, 2)], r_level.at[2, pl.ds(theirs, 2)], 0)
    halves[4].wait_recv()
    now = []
    for s in subs:
        down[0, s] = part(level, s, 4) + part(r_level, s, 3)
        now.append(remote(down.at[0, s], r_down.at[0, s], 4))
    level_grad(3, mine)
    both_grads(2)
    both_grads(1)
    level_grad(0, theirs)
    level_grad(0, mine)
    whole = remote(level.at[0], r_level0, 0)
    step_up(2)

    def masks():
        s_at = lax.broadcasted_iota(jnp.int32, (CHUNK, CHUNK), 0)
        t_at = lax.broadcasted_iota(jnp.int32, (CHUNK, CHUNK), 1)
        differ = jnp.bitwise_xor(s_at, t_at)

        @pl.loop(0, chunks)
        def _(n):
            full = jnp.zeros((CHUNK, CHUNK), F32)
            for m in range(8):
                line = codes[n, m : m + 1, :].astype(F32) * (factor(m) * scale)
                if m == 0:
                    full = jnp.broadcast_to(line, (CHUNK, CHUNK))
                else:
                    full = jnp.where(differ >= 1 << (m - 1), line, full)
            mask[n] = jnp.where(s_at <= t_at, full, 0.0)

    def inner_grads():
        weights(0, INNER)
        inner[7] = jnp.zeros(inner.shape[1:], F32)

        @pl.loop(0, heads)
        def _(h):
            found = []
            for b, _, (lo, hi) in PAIRS:
                query = qh[h, chunk(lo, hi - lo)].astype(F32)
                wide = (lam[chunk(lo, hi - lo), chunk(b)] * query).astype(BF16)
                found.append(scale * dot(gt[h, :, chunk(lo, hi - lo)], wide))
            for n in range(chunks - 1):
                parts = [found[m] for m, (_, (lo, hi), _) in enumerate(PAIRS) if lo <= n < hi]
                acc = parts[0]
                for x in parts[1:]:
                    acc = acc + x
                inner[n, h] = acc

    def diagonal(h, first, number):
        for n in range(first, first + number):
            rows = chunk(n)
            query, key, value, grad = qh[h, rows], kh[h, rows], vh[h, rows], gh[h, rows]
            weight_q = (mask[n] * dot(value, grad, NT)).astype(BF16)
            weight_v = (mask[n] * dot(key, query, NT)).astype(BF16)
            at = pl.ds(n * CHUNK * heads + h, CHUNK, stride=heads)
            flat_k[at, :] = dot(weight_q, query)
            flat_v[at, :] = dot(weight_v, grad)
            total = dot(weight_q, key, TN)
            grad32 = grad.astype(F32) * scale
            for m, (b, _, (lo, hi)) in enumerate(PAIRS):
                if lo <= n < hi:
                    wide = (lam[rows, chunk(b)] * grad32).astype(BF16)
                    total = total + dot(wide, states[m, h])
            dq[h, rows] = total

    def put_keys():
        put(flat_k, dk_out)
        put(flat_v, dv_out)
        put(inner, inner_out)

    def across(h):
        @pl.loop(0, 2)
        def _(i):
            rows = pl.ds(i * (count // 2), count // 2)
            grad32 = gh[h, rows].astype(F32) * scale
            wide = jnp.concatenate(
                [(lam[rows, chunk(INNER + b)] * grad32).astype(BF16) for b in range(CROSS)],
                axis=1)
            matrix = jnp.concatenate([cross[b, h] for b in range(CROSS)], axis=0)
            at = pl.ds(i * (heads * count // 2) + h, count // 2, stride=heads)
            tmp[at, :] = dq[h, rows] + dot(wide, matrix)

    def put_queries():
        flat[0] = tmp[...].astype(BF16)
        put(flat.at[0], dq_out)

    work = [masks, inner_grads]
    for h in range(heads):
        work.append(functools.partial(diagonal, h, 0, 4))
        work.append(functools.partial(diagonal, h, 4, 4))
    work.append(put_keys)
    work_after = [functools.partial(across, h) for h in range(heads)] + [put_queries]

    def do(queue, number=1):
        for _ in range(number):
            if queue:
                queue.pop(0)()

    found = []
    for n, b in enumerate((3, 2, 1)):
        halves[b].wait_recv()
        after = []
        for s in subs:
            now[s].wait_recv()
            value = r_down[n, s]
            if n:
                value = value + mid[n - 1, s]
            mid[n, s] = value
            down[n + 1, s] = value + part(level, s, b) + part(r_level, s, b - 1)
            after.append(remote(down.at[n + 1, s], r_down.at[n + 1, s], b))
            do(work)
        now = after
        if n == 0:
            step_up(3)
            for p in range(3):
                found.append(remote(r_tot.at[p], r_found.at[p], 0))
        if n == 1:
            for s in subs:
                up[3][s].wait_recv()
            found.append(remote(r_tot.at[3], r_found.at[3], 0))
    do(work, len(work))

    s_mine.wait_recv()
    for h in range(heads):
        cross[0, h] = r_state[h].astype(BF16)
    for p in range(4):
        found[p].wait_recv()
        for s in subs:
            rows = pl.ds(s % 2 * half, half)
            cross[p + 1, mine + s // 2, rows] = r_tot[p, s].astype(BF16)
            cross[p + 1, theirs + s // 2, rows] = r_found[p, s].astype(BF16)
    last = []
    for s in subs:
        now[s].wait_recv()
        mid[3, s] = mid[2, s] + r_down[3, s]
        last.append(remote(mid.at[3, s], r_mid.at[s], 0))
        do(work_after)
    do(work_after, len(work_after))

    whole.wait_recv()
    for s in subs:
        last[s].wait_recv()
        rows = pl.ds(s % 2 * half, half)
        i = s // 2
        ks_out[mine + i, rows] = mid[3, s] + r_level0[mine + i, rows]
        ks_out[theirs + i, rows] = r_mid[s] + r_level0[theirs + i, rows]

    for c in sent + codes_sent:
        c.wait_send()
    for c in outs:
        c.wait()


def exchange(scale, zs, heads, q, k, v, g, codes):
    count, width = q.shape[0] // heads, q.shape[1]
    chunks = count // CHUNK
    square = (width, width)
    piece = (4, 4, CHUNK // 2, width)
    any_space = pl.BlockSpec(memory_space=pl.ANY)
    vmem = pl.BlockSpec(memory_space=pltpu.VMEM)
    messages = 2 + 16 + 4 + 4 + 1 + 16 + 4
    return pl.pallas_call(
        functools.partial(exchange_kernel, scale, zs),
        out_shape=(
            jax.ShapeDtypeStruct((heads * count, width), BF16),
            jax.ShapeDtypeStruct((heads * count, width), F32),
            jax.ShapeDtypeStruct((heads * count, width), F32),
            jax.ShapeDtypeStruct((heads, *square), F32),
            jax.ShapeDtypeStruct((chunks, heads, *square), F32),
        ),
        in_specs=[any_space] * 5,
        out_specs=(any_space, any_space, any_space, vmem, any_space),
        scratch_shapes=[
            pltpu.VMEM((4, heads * count, width), BF16),
            pltpu.VMEM((heads * count, width), F32),
            *[pltpu.VMEM((heads, count, width), BF16)] * 4,
            pltpu.VMEM((heads, width, count), BF16),
            pltpu.VMEM((count, (INNER + CROSS) * width), F32),
            pltpu.VMEM((zs, ROWS, CHUNK), jnp.int32),
            pltpu.VMEM((chunks, *square), F32),
            pltpu.VMEM((len(PAIRS), heads, *square), BF16),
            pltpu.VMEM((chunks, heads, *square), F32),
            pltpu.VMEM((chunks, CHUNK, CHUNK), F32),
            pltpu.VMEM((heads, count, width), F32),
            pltpu.VMEM((heads * count, width), F32),
            pltpu.VMEM((heads * count, width), F32),
            pltpu.VMEM((CROSS, heads, *square), BF16),
            pltpu.VMEM((heads, *square), F32),
            pltpu.VMEM((heads, *square), F32),
            *[pltpu.VMEM(piece, F32)] * 3,
            pltpu.VMEM((CROSS, heads, *square), F32),
            pltpu.VMEM((4, heads, *square), F32),
            pltpu.VMEM((heads, *square), F32),
            *[pltpu.VMEM(piece, F32)] * 3,
            pltpu.VMEM(piece[1:], F32),
            pltpu.SemaphoreType.DMA((5,)),
            pltpu.SemaphoreType.DMA((4,)),
            pltpu.SemaphoreType.DMA((zs - 1,)),
            pltpu.SemaphoreType.DMA((zs - 1,)),
            pltpu.SemaphoreType.DMA((messages,)),
            pltpu.SemaphoreType.DMA((messages,)),
        ],
        compiler_params=pltpu.CompilerParams(
            collective_id=0, has_side_effects=True, vmem_limit_bytes=EXCHANGE_VMEM),
        name="exchange",
    )(q, k, v, g, codes)


EXCHANGE_VMEM = 60 << 20


def finish_kernel(k_in, v_in, dq_in, dk_in, dv_in, ks, inner, dq_out, dk_out, dv_out):
    heads = ks.shape[0]
    row = lax.broadcasted_iota(jnp.int32, (16, CHUNK), 0)
    keep = [
        (lax.rem(row, heads) == h).astype(F32).astype(BF16).reshape(1, 16, CHUNK)
        for h in range(heads)
    ]
    dq_out[...] = dq_in[...]
    steps = inner.shape[0]
    rows = heads * CHUNK
    for n in range(steps):
        at = pl.ds(n * rows, rows)
        total = [(ks[h] + inner[n, h]).astype(BF16) for h in range(heads)]

        def by_head(ref):
            x = ref[at, :].reshape(rows // 16, 16, CHUNK)
            return jnp.concatenate([(x * keep[h]).reshape(rows, CHUNK) for h in range(heads)], axis=1)

        dk = dot(by_head(v_in), jnp.concatenate(total, axis=0))
        dk_out[at, :] = (dk_in[at, :] + dk).astype(BF16)
        dv = dot(by_head(k_in), jnp.concatenate([x.T for x in total], axis=0))
        dv_out[at, :] = (dv_in[at, :] + dv).astype(BF16)


def finish(k, v, dq, dk, dv, ks, inner, steps=1):
    chunks, heads, width, _ = inner.shape
    block = pl.BlockSpec((steps * heads * CHUNK, width), lambda c: (c, 0))
    flat = jax.ShapeDtypeStruct(k.shape, BF16)
    return pl.pallas_call(
        finish_kernel,
        grid=(chunks // steps,),
        out_shape=(flat, flat, flat),
        in_specs=[block] * 5 + [
            pl.BlockSpec(memory_space=pltpu.VMEM),
            pl.BlockSpec((steps, heads, width, width), lambda c: (c, 0, 0, 0)),
        ],
        out_specs=(block,) * 3,
        compiler_params=pltpu.CompilerParams(vmem_limit_bytes=60 << 20),
        name="finish",
    )(k, v, dq, dk, dv, ks, inner)


def on_device(queries, keys, values, out_grad, level_codes):
    count, heads, width = queries.shape
    scale = width ** (-0.5)
    q, k, v, g = [x.reshape(count * heads, width) for x in (queries, keys, values, out_grad)]
    dq, dk, dv, ks, inner = exchange(
        scale, lax.axis_size("head"), heads, q, k, v, g, level_codes)
    grads = finish(k, v, dq, dk, dv, ks, inner)
    return tuple(x.reshape(count, heads, width) for x in grads)


def solution(mesh):
    return jax.shard_map(
        on_device,
        mesh=mesh,
        in_specs=(
            P("seq", "head", None),
            P("seq", "head", None),
            P("seq", "head", None),
            P("seq", "head", None),
            P(None, ("seq", "head")),
        ),
        out_specs=(P("seq", "head", None), P("seq", "head", None), P("seq", "head", None)),
        check_vma=False,
    )
```

```python
import functools

import jax
import jax.numpy as jnp
from jax import lax
from jax.experimental import pallas as pl
from jax.experimental.pallas import tpu as pltpu
from jax.sharding import PartitionSpec as P

MESH = pl.DeviceIdType.MESH
F32 = jnp.float32
BF16 = jnp.bfloat16
CHUNK = 128
INNER = 3
CROSS = 5
ROWS = 16
PARTNERS = (1, 2, 6, 8, 24)

NN = (((1,), (0,)), ((), ()))
NT = (((1,), (1,)), ((), ()))
TN = (((0,), (0,)), ((), ()))


def dot(a, b, dims=NN):
    return lax.dot_general(a, b, dims, preferred_element_type=F32)


def factor(level):
    return 2.0 ** (-0.5 * max(level - 1, 0)) / 16.0


def on_bit(index, bit):
    return lax.rem(jnp.right_shift(index, bit), 2).astype(F32)


def spread(codes, first, count):
    rows = lax.broadcasted_iota(jnp.int32, (codes.shape[0], count * CHUNK), 0)
    cols = lax.broadcasted_iota(jnp.int32, (codes.shape[0], count * CHUNK), 1)
    pick = (rows == first + jnp.right_shift(cols, 7)).astype(F32).astype(BF16)
    return dot(codes.astype(F32).astype(BF16), pick, TN)


def split_heads(flat, tmp, out):
    heads, count, _ = out.shape
    tmp[...] = flat[...].astype(F32)
    for h in range(heads):
        out[h] = tmp[pl.ds(h, count, stride=heads), :].astype(BF16)


def chunk(n, count=1):
    return pl.ds(n * CHUNK, count * CHUNK)


def total_of(items):
    items = list(items)
    acc = items[0]
    for x in items[1:]:
        acc = acc + x
    return acc


PAIRS = (
    (0, (0, 1), (1, 2)), (0, (2, 3), (3, 4)), (0, (4, 5), (5, 6)), (0, (6, 7), (7, 8)),
    (1, (0, 2), (2, 4)), (1, (4, 6), (6, 8)),
    (2, (0, 4), (4, 8)),
)


def exchange_kernel(
    scale, zs,
    q_in, k_in, v_in, g_in, codes_in,
    dq_out, dk_out, dv_out,
    flat, tmp, qh, kh, vh, gh, gt, lam, codes,
    one, states, inner, inner_t, mask, weight, dq, dk, dv, flat_k, flat_v, cross, ks,
    state, r_state, tot, r_tot, r_found,
    level, r_level, r_level0, down, r_down, mid, r_mid,
    in_sem, out_sem, code_send, code_recv, send, recv,
):
    seq = lax.axis_index("seq")
    z = lax.axis_index("head")
    mine = 2 * lax.rem(seq, 2)
    theirs = 2 - mine
    heads, count, width = qh.shape
    chunks = count // CHUNK
    subs = range(4)
    half = CHUNK // 2
    partner = [jnp.bitwise_xor(seq, p) for p in PARTNERS]

    barrier = pltpu.get_barrier_semaphore()
    for d in range(1, zs):
        pl.semaphore_signal(
            barrier, inc=1, device_id=(seq, lax.rem(z + d, zs)), device_id_type=MESH)
    for p in partner:
        pl.semaphore_signal(barrier, inc=1, device_id=(p, z), device_id_type=MESH)

    loads = [
        pltpu.make_async_copy(src, flat.at[i], in_sem.at[i])
        for i, src in enumerate((k_in, v_in, q_in, g_in))
    ]
    here = pltpu.make_async_copy(codes_in.at[pl.ds(0, ROWS)], codes.at[z], in_sem.at[4])
    for c in loads:
        c.start()
    here.start()

    sent = []

    def remote(src, dst, to):
        n = len(sent)
        c = pltpu.make_async_remote_copy(
            src_ref=src, dst_ref=dst, send_sem=send.at[n], recv_sem=recv.at[n],
            device_id=(partner[to], z), device_id_type=MESH)
        sent.append(c)
        c.start()
        return c

    outs = []

    def put(src, dst):
        c = pltpu.make_async_copy(src, dst, out_sem.at[len(outs)])
        c.start()
        outs.append(c)

    loads[0].wait()
    split_heads(flat.at[0], tmp, kh)
    loads[1].wait()
    split_heads(flat.at[1], tmp, vh)
    here.wait()

    @pl.loop(0, heads // 2)
    def _(pair):
        for i in range(2):
            h = 2 * pair + i
            for n in range(chunks):
                one[i, n] = dot(vh[h, chunk(n)], kh[h, chunk(n)], TN)
            state[h] = total_of(one[i, n] for n in range(chunks))
            for m, (b, (lo, hi), _) in enumerate(PAIRS):
                acc = total_of(one[i, n] for n in range(lo, hi))
                states[m, h] = (acc * (scale * factor(8 + b))).astype(BF16)

    pl.semaphore_wait(barrier, len(partner) + zs - 1)
    codes_sent = []
    for d in range(1, zs):
        c = pltpu.make_async_remote_copy(
            src_ref=codes_in.at[pl.ds(0, ROWS)], dst_ref=codes.at[z],
            send_sem=code_send.at[d - 1], recv_sem=code_recv.at[d - 1],
            device_id=(seq, lax.rem(z + d, zs)), device_id_type=MESH)
        c.start()
        codes_sent.append(c)
    s_their = remote(state.at[pl.ds(theirs, 2)], r_state.at[pl.ds(theirs, 2)], 0)
    s_mine = remote(state.at[pl.ds(mine, 2)], r_state.at[pl.ds(mine, 2)], 0)

    def part(ref, s, *lead):
        return ref[(*lead, mine + s // 2, pl.ds(s % 2 * half, half))]

    loads[3].wait()
    split_heads(flat.at[3], tmp, gh)

    s_their.wait_recv()
    up = [[]]
    for s in subs:
        tot[0, s] = part(state, s) + part(r_state, s)
        up[0].append(remote(tot.at[0, s], r_tot.at[0, s], 1))

    loads[2].wait()
    split_heads(flat.at[2], tmp, qh)
    for h in range(heads):
        for n in range(chunks):
            gt[h, :, chunk(n)] = gh[h, chunk(n)].T

    def step_up(p):
        up.append([])
        for s in subs:
            up[p - 1][s].wait_recv()
            tot[p, s] = tot[p - 1, s] + r_tot[p - 1, s]
            up[p].append(remote(tot.at[p, s], r_tot.at[p, s], p + 1))

    def spread_codes(first, number):
        for c in range(chunks):
            lam[chunk(c), chunk(first, number)] = spread(codes[c], 8 + first, number).astype(BF16)

    def level_grads(bits, h):
        wide = jnp.concatenate([lam[:, chunk(INNER + b)] * qh[h] for b in bits], axis=1)
        result = dot(gt[h], wide)
        for i, b in enumerate(bits):
            level[b, h] = (scale * factor(11 + b) * on_bit(seq, b)) * result[
                :, i * CHUNK : (i + 1) * CHUNK]

    halves = [None] * CROSS

    def send_half(b):
        halves[b] = remote(
            level.at[b, pl.ds(theirs, 2)], r_level.at[b - 1, pl.ds(theirs, 2)], 0)

    for c in codes_sent:
        c.wait_recv()
    spread_codes(INNER + 3, 2)
    for i in range(2):
        level_grads((3, 4), theirs + i)
    send_half(4)
    send_half(3)
    for i in range(2):
        level_grads((3, 4), mine + i)
    step_up(1)
    spread_codes(0, INNER + 3)
    halves[4].wait_recv()
    now = []
    for s in subs:
        down[0, s] = part(level, s, 4) + part(r_level, s, 3)
        now.append(remote(down.at[0, s], r_down.at[0, s], 4))
    for i in range(2):
        level_grads((0, 1, 2), theirs + i)
    send_half(2)
    send_half(1)
    for i in range(2):
        level_grads((0, 1, 2), mine + i)
    whole = remote(level.at[0], r_level0, 0)
    step_up(2)

    def masks():
        s_at = lax.broadcasted_iota(jnp.int32, (CHUNK, CHUNK), 0)
        t_at = lax.broadcasted_iota(jnp.int32, (CHUNK, CHUNK), 1)
        differ = jnp.bitwise_xor(s_at, t_at)

        @pl.loop(0, chunks)
        def _(n):
            full = jnp.zeros((CHUNK, CHUNK), F32)
            for m in range(8):
                line = codes[n, m : m + 1, :].astype(F32) * (factor(m) * scale)
                if m == 0:
                    full = jnp.broadcast_to(line, (CHUNK, CHUNK))
                else:
                    full = jnp.where(differ >= 1 << (m - 1), line, full)
            mask[n] = jnp.where(s_at <= t_at, full, 0.0)

    def inner_grads(first):
        for h in range(first, first + 2):
            found = []
            for b, _, (lo, hi) in PAIRS:
                rows = chunk(lo, hi - lo)
                wide = lam[rows, chunk(b)] * qh[h, rows]
                found.append((scale * factor(8 + b)) * dot(gt[h, :, rows], wide))
            for n in range(chunks - 1):
                acc = total_of(
                    found[m] for m, (_, (lo, hi), _) in enumerate(PAIRS) if lo <= n < hi)
                value = acc.astype(BF16)
                inner[n, h] = value
                inner_t[n, h] = value.T

    def first_stage(u):
        h, start = u // 2, u % 2 * 4
        for i in range(4):
            rows = chunk(start + i)
            weights = mask[start + i]
            weight[u % 2, i, 0] = (weights * dot(vh[h, rows], gh[h, rows], NT)).astype(BF16)
            weight[u % 2, i, 1] = (weights * dot(kh[h, rows], qh[h, rows], NT)).astype(BF16)

    def second_stage(u):
        h, start = u // 2, u % 2 * 4
        for i in range(4):
            n = start + i
            rows = chunk(n)
            query, key, value, grad = qh[h, rows], kh[h, rows], vh[h, rows], gh[h, rows]
            weight_q, weight_v = weight[u % 2, i, 0], weight[u % 2, i, 1]
            if n < chunks - 1:
                dk[h, rows] = dot(
                    jnp.concatenate([weight_q, value], axis=1),
                    jnp.concatenate([query, inner[n, h]], axis=0))
                dv[h, rows] = dot(
                    jnp.concatenate([weight_v, key], axis=1),
                    jnp.concatenate([grad, inner_t[n, h]], axis=0))
            else:
                dk[h, rows] = dot(weight_q, query)
                dv[h, rows] = dot(weight_v, grad)
            left, right = [weight_q.T], [key]
            for m, (b, _, (lo, hi)) in enumerate(PAIRS):
                if lo <= n < hi:
                    left.append(lam[rows, chunk(b)] * grad)
                    right.append(states[m, h])
            dq[h, rows] = dot(jnp.concatenate(left, axis=1), jnp.concatenate(right, axis=0))

    def diagonal(u):
        if u > 0:
            second_stage(u - 1)
        if u < 8:
            first_stage(u)

    def across(h):
        wide = jnp.concatenate([lam[:, chunk(INNER + b)] * gh[h] for b in range(CROSS)], axis=1)
        matrix = jnp.concatenate([cross[b, h] for b in range(CROSS)], axis=0)
        tmp[pl.ds(h, count, stride=heads), :] = dq[h] + dot(wide, matrix)

    def put_queries():
        flat[0] = tmp[...].astype(BF16)
        put(flat.at[0], dq_out)

    def finish(h):
        at = pl.ds(h, count, stride=heads)
        flat_k[at, :] = dk[h] + dot(vh[h], ks[h])
        flat_v[at, :] = dv[h] + dot(kh[h], ks[h], NT)

    work = [masks, functools.partial(inner_grads, 0), functools.partial(inner_grads, 2)]
    work += [functools.partial(diagonal, u) for u in range(9)]

    def do(number=1):
        for _ in range(number):
            if work:
                work.pop(0)()

    found = []
    for n, b in enumerate((3, 2, 1)):
        halves[b].wait_recv()
        after = []
        for s in subs:
            now[s].wait_recv()
            value = r_down[n, s]
            if n:
                value = value + mid[n - 1, s]
            mid[n, s] = value
            down[n + 1, s] = value + part(level, s, b) + part(r_level, s, b - 1)
            after.append(remote(down.at[n + 1, s], r_down.at[n + 1, s], b))
            do()
        now = after
        if n == 0:
            step_up(3)
            for p in range(3):
                found.append(remote(r_tot.at[p], r_found.at[p], 0))
        if n == 1:
            for s in subs:
                up[3][s].wait_recv()
            found.append(remote(r_tot.at[3], r_found.at[3], 0))
    do(len(work))

    s_mine.wait_recv()
    for h in range(heads):
        cross[0, h] = ((scale * factor(11)) * on_bit(seq, 0) * r_state[h]).astype(BF16)
    for p in range(4):
        found[p].wait_recv()
        value = (scale * factor(12 + p)) * on_bit(seq, p + 1)
        for s in subs:
            rows = pl.ds(s % 2 * half, half)
            cross[p + 1, mine + s // 2, rows] = (value * r_tot[p, s]).astype(BF16)
            cross[p + 1, theirs + s // 2, rows] = (value * r_found[p, s]).astype(BF16)
    for h in range(heads):
        across(h)
    put_queries()

    last = []
    whole.wait_recv()
    for s in subs:
        now[s].wait_recv()
        mid[3, s] = mid[2, s] + r_down[3, s]
        last.append(remote(mid.at[3, s], r_mid.at[s], 0))
        rows = pl.ds(s % 2 * half, half)
        ks[mine + s // 2, rows] = (mid[3, s] + part(r_level0, s)).astype(BF16)
        if s % 2:
            finish(mine + s // 2)
    for s in subs:
        last[s].wait_recv()
        rows = pl.ds(s % 2 * half, half)
        ks[theirs + s // 2, rows] = (r_mid[s] + r_level0[theirs + s // 2, rows]).astype(BF16)
    for i in range(2):
        finish(theirs + i)
    flat[1] = flat_k[...].astype(BF16)
    put(flat.at[1], dk_out)
    flat[2] = flat_v[...].astype(BF16)
    put(flat.at[2], dv_out)

    for c in sent + codes_sent:
        c.wait_send()
    for c in outs:
        c.wait()


def exchange(scale, zs, heads, q, k, v, g, codes):
    count, width = q.shape[0] // heads, q.shape[1]
    chunks = count // CHUNK
    square = (width, width)
    piece = (4, 4, CHUNK // 2, width)
    any_space = pl.BlockSpec(memory_space=pl.ANY)
    messages = 2 + 16 + 4 + 4 + 1 + 16 + 4
    flat = jax.ShapeDtypeStruct((heads * count, width), BF16)
    return pl.pallas_call(
        functools.partial(exchange_kernel, scale, zs),
        out_shape=(flat,) * 3,
        in_specs=[any_space] * 5,
        out_specs=(any_space,) * 3,
        scratch_shapes=[
            pltpu.VMEM((4, heads * count, width), BF16),
            pltpu.VMEM((heads * count, width), F32),
            *[pltpu.VMEM((heads, count, width), BF16)] * 4,
            pltpu.VMEM((heads, width, count), BF16),
            pltpu.VMEM((count, (INNER + CROSS) * width), BF16),
            pltpu.VMEM((zs, ROWS, CHUNK), jnp.int32),
            pltpu.VMEM((2, chunks, *square), F32),
            pltpu.VMEM((len(PAIRS), heads, *square), BF16),
            *[pltpu.VMEM((chunks - 1, heads, *square), BF16)] * 2,
            pltpu.VMEM((chunks, CHUNK, CHUNK), F32),
            pltpu.VMEM((2, 4, 2, CHUNK, CHUNK), BF16),
            *[pltpu.VMEM((heads, count, width), F32)] * 3,
            *[pltpu.VMEM((heads * count, width), F32)] * 2,
            pltpu.VMEM((CROSS, heads, *square), BF16),
            pltpu.VMEM((heads, *square), BF16),
            pltpu.VMEM((heads, *square), F32),
            pltpu.VMEM((heads, *square), F32),
            *[pltpu.VMEM(piece, F32)] * 3,
            pltpu.VMEM((CROSS, heads, *square), F32),
            pltpu.VMEM((4, heads, *square), F32),
            pltpu.VMEM((heads, *square), F32),
            *[pltpu.VMEM(piece, F32)] * 3,
            pltpu.VMEM(piece[1:], F32),
            pltpu.SemaphoreType.DMA((5,)),
            pltpu.SemaphoreType.DMA((3,)),
            pltpu.SemaphoreType.DMA((zs - 1,)),
            pltpu.SemaphoreType.DMA((zs - 1,)),
            pltpu.SemaphoreType.DMA((messages,)),
            pltpu.SemaphoreType.DMA((messages,)),
        ],
        compiler_params=pltpu.CompilerParams(
            collective_id=0, has_side_effects=True, vmem_limit_bytes=60 << 20),
        name="exchange",
    )(q, k, v, g, codes)


def on_device(queries, keys, values, out_grad, level_codes):
    count, heads, width = queries.shape
    scale = width ** (-0.5)
    flat = [x.reshape(count * heads, width) for x in (queries, keys, values, out_grad)]
    grads = exchange(scale, lax.axis_size("head"), heads, *flat, level_codes)
    return tuple(x.reshape(count, heads, width) for x in grads)


def solution(mesh):
    return jax.shard_map(
        on_device,
        mesh=mesh,
        in_specs=(
            P("seq", "head", None),
            P("seq", "head", None),
            P("seq", "head", None),
            P("seq", "head", None),
            P(None, ("seq", "head")),
        ),
        out_specs=(P("seq", "head", None), P("seq", "head", None), P("seq", "head", None)),
        check_vma=False,
    )
```

```python
import functools

import jax
import jax.numpy as jnp
from jax import lax
from jax.experimental import pallas as pl
from jax.experimental.pallas import tpu as pltpu
from jax.sharding import PartitionSpec as P

MESH = pl.DeviceIdType.MESH
F32 = jnp.float32
BF16 = jnp.bfloat16
CHUNK = 128
INNER = 3
CROSS = 5
ROWS = 16
PARTNERS = (1, 2, 6, 8, 24)

NN = (((1,), (0,)), ((), ()))
NT = (((1,), (1,)), ((), ()))
TN = (((0,), (0,)), ((), ()))


def dot(a, b, dims=NN):
    return lax.dot_general(a, b, dims, preferred_element_type=F32)


def factor(level):
    return 2.0 ** (-0.5 * max(level - 1, 0)) / 16.0


def on_bit(index, bit):
    return lax.rem(jnp.right_shift(index, bit), 2).astype(F32)


def split_heads(flat, tmp, out):
    heads, count, _ = out.shape
    tmp[...] = flat[...].astype(F32)
    for h in range(heads):
        out[h] = tmp[pl.ds(h, count, stride=heads), :].astype(BF16)


def chunk(n, count=1):
    return pl.ds(n * CHUNK, count * CHUNK)


def total_of(items):
    items = list(items)
    acc = items[0]
    for x in items[1:]:
        acc = acc + x
    return acc


PAIRS = (
    (0, (0, 1), (1, 2)), (0, (2, 3), (3, 4)), (0, (4, 5), (5, 6)), (0, (6, 7), (7, 8)),
    (1, (0, 2), (2, 4)), (1, (4, 6), (6, 8)),
    (2, (0, 4), (4, 8)),
)


def exchange_kernel(
    scale, zs,
    q_in, k_in, v_in, g_in, codes_in,
    flat_q, flat_k, flat_v,
    flat, tmp, qh, kh, vh, gh, qt, kt, gt, lam, codes,
    one, states, inner, inner_t, mask, weight, dq, dk, dv, cross, ks,
    state, r_state, tot, r_tot, r_found,
    level, r_level, r_level0, down, r_down, mid, r_mid,
    in_sem, code_send, code_recv, send, recv,
):
    seq = lax.axis_index("seq")
    z = lax.axis_index("head")
    mine = 2 * lax.rem(seq, 2)
    theirs = 2 - mine
    heads, count, width = qh.shape
    chunks = count // CHUNK
    subs = range(4)
    half = CHUNK // 2
    partner = [jnp.bitwise_xor(seq, p) for p in PARTNERS]

    barrier = pltpu.get_barrier_semaphore()
    for d in range(1, zs):
        pl.semaphore_signal(
            barrier, inc=1, device_id=(seq, lax.rem(z + d, zs)), device_id_type=MESH)
    for p in partner:
        pl.semaphore_signal(barrier, inc=1, device_id=(p, z), device_id_type=MESH)

    loads = [
        pltpu.make_async_copy(src, flat.at[i], in_sem.at[i])
        for i, src in enumerate((k_in, v_in, q_in, g_in))
    ]
    here = pltpu.make_async_copy(codes_in.at[pl.ds(0, ROWS)], codes.at[z], in_sem.at[4])
    for c in loads:
        c.start()
    here.start()

    sent = []

    def remote(src, dst, to):
        n = len(sent)
        c = pltpu.make_async_remote_copy(
            src_ref=src, dst_ref=dst, send_sem=send.at[n], recv_sem=recv.at[n],
            device_id=(partner[to], z), device_id_type=MESH)
        sent.append(c)
        c.start()
        return c

    def transpose(src, dst):
        for h in range(heads):
            for n in range(chunks):
                dst[h, :, chunk(n)] = src[h, chunk(n)].T

    loads[0].wait()
    split_heads(flat.at[0], tmp, kh)
    transpose(kh, kt)
    loads[1].wait()
    split_heads(flat.at[1], tmp, vh)
    here.wait()

    @pl.loop(0, heads // 2)
    def _(pair):
        for i in range(2):
            h = 2 * pair + i
            for n in range(chunks):
                one[i, n] = dot(kt[h, :, chunk(n)], vh[h, chunk(n)])
            state[h] = total_of(one[i, n] for n in range(chunks))
            for m, (b, (lo, hi), _) in enumerate(PAIRS):
                acc = total_of(one[i, n] for n in range(lo, hi))
                states[m, h] = (acc * (scale * factor(8 + b))).astype(BF16)

    pl.semaphore_wait(barrier, len(partner) + zs - 1)
    codes_sent = []
    for d in range(1, zs):
        c = pltpu.make_async_remote_copy(
            src_ref=codes_in.at[pl.ds(0, ROWS)], dst_ref=codes.at[z],
            send_sem=code_send.at[d - 1], recv_sem=code_recv.at[d - 1],
            device_id=(seq, lax.rem(z + d, zs)), device_id_type=MESH)
        c.start()
        codes_sent.append(c)
    s_their = remote(state.at[pl.ds(theirs, 2)], r_state.at[pl.ds(theirs, 2)], 0)
    s_mine = remote(state.at[pl.ds(mine, 2)], r_state.at[pl.ds(mine, 2)], 0)

    def part(ref, s, *lead):
        return ref[(*lead, mine + s // 2, pl.ds(s % 2 * half, half))]

    loads[3].wait()
    split_heads(flat.at[3], tmp, gh)
    transpose(gh, gt)

    s_their.wait_recv()
    up = [[]]
    for s in subs:
        tot[0, s] = part(state, s) + part(r_state, s)
        up[0].append(remote(tot.at[0, s], r_tot.at[0, s], 1))

    loads[2].wait()
    split_heads(flat.at[2], tmp, qh)
    transpose(qh, qt)

    def step_up(p):
        up.append([])
        for s in subs:
            up[p - 1][s].wait_recv()
            tot[p, s] = tot[p - 1, s] + r_tot[p - 1, s]
            up[p].append(remote(tot.at[p, s], r_tot.at[p, s], p + 1))

    def code_rows():
        for m in range(INNER + CROSS):
            for c in range(chunks):
                line = codes[c, 8 + m : 9 + m, :].astype(F32)
                lam[m, :, chunk(c)] = jnp.broadcast_to(line, (16, CHUNK)).astype(BF16)

    def by_code(m, matrix, rows):
        tiles = matrix.reshape(matrix.shape[0] // 16, 16, matrix.shape[1])
        return (tiles * lam[m, :, rows][None]).reshape(matrix.shape)

    everything = pl.ds(0, count)

    def level_grads(bits, h):
        query = qt[h]
        tall = jnp.concatenate([by_code(INNER + b, query, everything) for b in bits], axis=0)
        result = dot(tall, gh[h])
        for i, b in enumerate(bits):
            level[b, h] = (scale * factor(11 + b) * on_bit(seq, b)) * result[
                i * CHUNK : (i + 1) * CHUNK]

    halves = [None] * CROSS

    def send_half(b):
        halves[b] = remote(
            level.at[b, pl.ds(theirs, 2)], r_level.at[b - 1, pl.ds(theirs, 2)], 0)

    for c in codes_sent:
        c.wait_recv()
    code_rows()
    for i in range(2):
        level_grads(range(CROSS), theirs + i)
    for b in (4, 3, 2, 1):
        send_half(b)
    for i in range(2):
        level_grads(range(CROSS), mine + i)
    whole = remote(level.at[0], r_level0, 0)
    step_up(1)
    halves[4].wait_recv()
    now = []
    for s in subs:
        down[0, s] = part(level, s, 4) + part(r_level, s, 3)
        now.append(remote(down.at[0, s], r_down.at[0, s], 4))
    step_up(2)

    def masks():
        s_at = lax.broadcasted_iota(jnp.int32, (CHUNK, CHUNK), 0)
        t_at = lax.broadcasted_iota(jnp.int32, (CHUNK, CHUNK), 1)
        differ = jnp.bitwise_xor(s_at, t_at)

        @pl.loop(0, chunks)
        def _(n):
            full = jnp.zeros((CHUNK, CHUNK), F32)
            for m in range(8):
                line = codes[n, m : m + 1, :].astype(F32) * (factor(m) * scale)
                if m == 0:
                    full = jnp.broadcast_to(line, (CHUNK, CHUNK))
                else:
                    full = jnp.where(differ >= 1 << (m - 1), line, full)
            mask[n] = jnp.where(s_at <= t_at, full, 0.0)

    def inner_grads(first):
        for h in range(first, first + 2):
            found = []
            for b, _, (lo, hi) in PAIRS:
                rows = chunk(lo, hi - lo)
                tall = by_code(b, qt[h, :, rows], rows)
                found.append((scale * factor(8 + b)) * dot(tall, gh[h, rows]))
            for n in range(chunks - 1):
                acc = total_of(
                    found[m] for m, (_, (lo, hi), _) in enumerate(PAIRS) if lo <= n < hi)
                value = acc.astype(BF16)
                inner[n, h] = value
                inner_t[n, h] = value.T

    def first_stage(u):
        h, start = u // 2, u % 2 * 4
        for i in range(4):
            rows = chunk(start + i)
            weights = mask[start + i]
            weight[u % 2, i, 0] = (weights * dot(vh[h, rows], gt[h, :, rows])).astype(BF16)
            weight[u % 2, i, 1] = (weights * dot(kh[h, rows], qt[h, :, rows])).astype(BF16)

    def second_stage(u):
        h, start = u // 2, u % 2 * 4
        for i in range(4):
            n = start + i
            rows = chunk(n)
            query, key, value, grad = qh[h, rows], kh[h, rows], vh[h, rows], gh[h, rows]
            weight_q, weight_v = weight[u % 2, i, 0], weight[u % 2, i, 1]
            if n < chunks - 1:
                dk[h, rows] = dot(
                    jnp.concatenate([weight_q, value], axis=1),
                    jnp.concatenate([query, inner_t[n, h]], axis=0))
                dv[h, rows] = dot(
                    jnp.concatenate([weight_v, key], axis=1),
                    jnp.concatenate([grad, inner[n, h]], axis=0))
            else:
                dk[h, rows] = dot(weight_q, query)
                dv[h, rows] = dot(weight_v, grad)
            left, right = [kt[h, :, rows]], [weight_q]
            for m, (b, _, (lo, hi)) in enumerate(PAIRS):
                if lo <= n < hi:
                    left.append(states[m, h])
                    right.append(by_code(b, gt[h, :, rows], rows))
            dq[h, :, rows] = dot(jnp.concatenate(left, axis=1), jnp.concatenate(right, axis=0))

    def diagonal(u):
        if u > 0:
            second_stage(u - 1)
        if u < 8:
            first_stage(u)

    def across(h):
        matrix = jnp.concatenate([cross[b, h] for b in range(CROSS)], axis=1)
        for n in range(0, chunks, 2):
            rows = chunk(n, 2)
            grad = gt[h, :, rows]
            tall = jnp.concatenate([by_code(INNER + b, grad, rows) for b in range(CROSS)], axis=0)
            result = (dq[h, :, rows] + dot(matrix, tall)).astype(BF16)
            for i in range(2):
                at = pl.ds((n + i) * CHUNK * heads + h, CHUNK, stride=heads)
                flat_q[at, :] = result[:, i * CHUNK : (i + 1) * CHUNK].T.astype(F32)

    def finish(h):
        at = pl.ds(h, count, stride=heads)
        matrix, zero = ks[h], jnp.zeros((CHUNK, CHUNK), BF16)
        both = jnp.concatenate([
            jnp.concatenate([matrix.T, zero], axis=1),
            jnp.concatenate([zero, matrix], axis=1)], axis=0)
        result = dot(jnp.concatenate([vh[h], kh[h]], axis=1), both)
        flat_k[at, :] = dk[h] + result[:, :CHUNK]
        flat_v[at, :] = dv[h] + result[:, CHUNK:]

    work = [masks, functools.partial(inner_grads, 0), functools.partial(inner_grads, 2)]
    work += [functools.partial(diagonal, u) for u in range(9)]

    def do(number=1):
        for _ in range(number):
            if work:
                work.pop(0)()

    found = []
    for n, b in enumerate((3, 2, 1)):
        halves[b].wait_recv()
        after = []
        for s in subs:
            now[s].wait_recv()
            value = r_down[n, s]
            if n:
                value = value + mid[n - 1, s]
            mid[n, s] = value
            down[n + 1, s] = value + part(level, s, b) + part(r_level, s, b - 1)
            after.append(remote(down.at[n + 1, s], r_down.at[n + 1, s], b))
            do()
        now = after
        if n == 0:
            step_up(3)
            for p in range(3):
                found.append(remote(r_tot.at[p], r_found.at[p], 0))
        if n == 1:
            for s in subs:
                up[3][s].wait_recv()
            found.append(remote(r_tot.at[3], r_found.at[3], 0))
    do(len(work))

    s_mine.wait_recv()
    for h in range(heads):
        cross[0, h] = ((scale * factor(11)) * on_bit(seq, 0) * r_state[h]).astype(BF16)
    for p in range(4):
        found[p].wait_recv()
        value = (scale * factor(12 + p)) * on_bit(seq, p + 1)
        for s in subs:
            rows = pl.ds(s % 2 * half, half)
            cross[p + 1, mine + s // 2, rows] = (value * r_tot[p, s]).astype(BF16)
            cross[p + 1, theirs + s // 2, rows] = (value * r_found[p, s]).astype(BF16)
    for h in range(heads):
        across(h)

    last = []
    whole.wait_recv()
    for s in subs:
        now[s].wait_recv()
        mid[3, s] = mid[2, s] + r_down[3, s]
        last.append(remote(mid.at[3, s], r_mid.at[s], 0))
        rows = pl.ds(s % 2 * half, half)
        ks[mine + s // 2, rows] = (mid[3, s] + part(r_level0, s)).astype(BF16)
    for i in range(2):
        finish(mine + i)
    for s in subs:
        last[s].wait_recv()
        rows = pl.ds(s % 2 * half, half)
        ks[theirs + s // 2, rows] = (r_mid[s] + r_level0[theirs + s // 2, rows]).astype(BF16)
    for i in range(2):
        finish(theirs + i)

    for c in sent + codes_sent:
        c.wait_send()


def exchange(scale, zs, heads, q, k, v, g, codes):
    count, width = q.shape[0] // heads, q.shape[1]
    chunks = count // CHUNK
    square = (width, width)
    piece = (4, 4, CHUNK // 2, width)
    hbm = pl.BlockSpec(memory_space=pltpu.HBM)
    vmem = pl.BlockSpec(memory_space=pltpu.VMEM)
    messages = 2 + 16 + 4 + 4 + 1 + 16 + 4
    flat = jax.ShapeDtypeStruct((heads * count, width), F32)
    return pl.pallas_call(
        functools.partial(exchange_kernel, scale, zs),
        out_shape=(flat,) * 3,
        in_specs=[hbm] * 5,
        out_specs=(vmem,) * 3,
        scratch_shapes=[
            pltpu.VMEM((4, heads * count, width), BF16),
            pltpu.VMEM((heads * count, width), F32),
            *[pltpu.VMEM((heads, count, width), BF16)] * 4,
            *[pltpu.VMEM((heads, width, count), BF16)] * 3,
            pltpu.VMEM((INNER + CROSS, 16, count), BF16),
            pltpu.VMEM((zs, ROWS, CHUNK), jnp.int32),
            pltpu.VMEM((2, chunks, *square), F32),
            pltpu.VMEM((len(PAIRS), heads, *square), BF16),
            *[pltpu.VMEM((chunks - 1, heads, *square), BF16)] * 2,
            pltpu.VMEM((chunks, CHUNK, CHUNK), F32),
            pltpu.VMEM((2, 4, 2, CHUNK, CHUNK), BF16),
            pltpu.VMEM((heads, width, count), F32),
            *[pltpu.VMEM((heads, count, width), F32)] * 2,
            pltpu.VMEM((CROSS, heads, *square), BF16),
            pltpu.VMEM((heads, *square), BF16),
            pltpu.VMEM((heads, *square), F32),
            pltpu.VMEM((heads, *square), F32),
            *[pltpu.VMEM(piece, F32)] * 3,
            pltpu.VMEM((CROSS, heads, *square), F32),
            pltpu.VMEM((4, heads, *square), F32),
            pltpu.VMEM((heads, *square), F32),
            *[pltpu.VMEM(piece, F32)] * 3,
            pltpu.VMEM(piece[1:], F32),
            pltpu.SemaphoreType.DMA((5,)),
            pltpu.SemaphoreType.DMA((zs - 1,)),
            pltpu.SemaphoreType.DMA((zs - 1,)),
            pltpu.SemaphoreType.DMA((messages,)),
            pltpu.SemaphoreType.DMA((messages,)),
        ],
        compiler_params=pltpu.CompilerParams(
            collective_id=0, has_side_effects=True, vmem_limit_bytes=LIMIT),
        name="exchange",
    )(q, k, v, g, codes)


LIMIT = 44 << 20


def pack_kernel(q_in, k_in, v_in, q_out, k_out, v_out, stage, sem):
    rows = q_in.shape[0] // 4
    copies = []
    for i, (src, dst) in enumerate(((q_in, q_out), (k_in, k_out), (v_in, v_out))):
        for n in range(4):
            at = pl.ds(n * rows, rows)
            stage[i, at] = src[at, :].astype(BF16)
            c = pltpu.make_async_copy(stage.at[i, at], dst.at[at], sem.at[i, n])
            c.start()
            copies.append(c)
    for c in copies:
        c.wait()


def pack(*flat):
    shape = flat[0].shape
    return pl.pallas_call(
        pack_kernel,
        out_shape=(jax.ShapeDtypeStruct(shape, BF16),) * 3,
        in_specs=[pl.BlockSpec(memory_space=pltpu.VMEM)] * 3,
        out_specs=(pl.BlockSpec(memory_space=pltpu.HBM),) * 3,
        scratch_shapes=[pltpu.VMEM((3, *shape), BF16), pltpu.SemaphoreType.DMA((3, 4))],
        compiler_params=pltpu.CompilerParams(vmem_limit_bytes=16 << 20),
        name="pack",
    )(*flat)


def on_device(queries, keys, values, out_grad, level_codes):
    count, heads, width = queries.shape
    scale = width ** (-0.5)
    flat = [x.reshape(count * heads, width) for x in (queries, keys, values, out_grad)]
    flat = [pltpu.with_memory_space_constraint(x, pltpu.HBM) for x in flat]
    grads = pack(*exchange(scale, lax.axis_size("head"), heads, *flat, level_codes))
    return tuple(x.reshape(count, heads, width) for x in grads)


def solution(mesh):
    return jax.shard_map(
        on_device,
        mesh=mesh,
        in_specs=(
            P("seq", "head", None),
            P("seq", "head", None),
            P("seq", "head", None),
            P("seq", "head", None),
            P(None, ("seq", "head")),
        ),
        out_specs=(P("seq", "head", None), P("seq", "head", None), P("seq", "head", None)),
        check_vma=False,
    )
```

```python
import functools

import jax
import jax.numpy as jnp
from jax import lax
from jax.experimental import pallas as pl
from jax.experimental.pallas import tpu as pltpu
from jax.sharding import PartitionSpec as P

MESH = pl.DeviceIdType.MESH
F32 = jnp.float32
BF16 = jnp.bfloat16
CHUNK = 128
INNER = 3
CROSS = 5
ROWS = 16
SPLIT = 2
PARTNERS = (1, 2, 6, 8, 24)

NN = (((1,), (0,)), ((), ()))
NT = (((1,), (1,)), ((), ()))
TN = (((0,), (0,)), ((), ()))


def dot(a, b, dims=NN):
    return lax.dot_general(a, b, dims, preferred_element_type=F32)


def factor(level):
    return 2.0 ** (-0.5 * max(level - 1, 0)) / 16.0


def on_bit(index, bit):
    return lax.rem(jnp.right_shift(index, bit), 2).astype(F32)


def split_heads(flat, tmp, out):
    heads, count, _ = out.shape
    tmp[...] = flat[...].astype(F32)
    for h in range(heads):
        out[h] = tmp[pl.ds(h, count, stride=heads), :].astype(BF16)


def chunk(n, count=1):
    return pl.ds(n * CHUNK, count * CHUNK)


def total_of(items):
    items = list(items)
    acc = items[0]
    for x in items[1:]:
        acc = acc + x
    return acc


PAIRS = (
    (0, (0, 1), (1, 2)), (0, (2, 3), (3, 4)), (0, (4, 5), (5, 6)), (0, (6, 7), (7, 8)),
    (1, (0, 2), (2, 4)), (1, (4, 6), (6, 8)),
    (2, (0, 4), (4, 8)),
)


def exchange_kernel(
    scale, zs,
    q_in, k_in, v_in, g_in, codes_in,
    flat_q, flat_k, flat_v,
    flat, tmp, qh, kh, vh, gh, qt, kt, gt, lam, codes,
    one, states, inner, inner_t, mask, weight, dq, dk, dv, cross, ks,
    state, r_state, tot, r_tot, r_found,
    level, r_level, r_level0, down, r_down, mid, r_mid,
    in_sem, code_send, code_recv, send, recv,
):
    seq = lax.axis_index("seq")
    z = lax.axis_index("head")
    mine = 2 * lax.rem(seq, 2)
    theirs = 2 - mine
    heads, count, width = qh.shape
    chunks = count // CHUNK
    subs = range(2 * SPLIT)
    half = CHUNK // SPLIT
    partner = [jnp.bitwise_xor(seq, p) for p in PARTNERS]

    loads = [
        pltpu.make_async_copy(src, flat.at[i], in_sem.at[i])
        for i, src in enumerate((k_in, v_in, q_in, g_in))
    ]
    here = pltpu.make_async_copy(codes_in.at[pl.ds(0, ROWS)], codes.at[z], in_sem.at[4])
    loads[0].start()
    barrier = pltpu.get_barrier_semaphore()
    for d in range(1, zs):
        pl.semaphore_signal(
            barrier, inc=1, device_id=(seq, lax.rem(z + d, zs)), device_id_type=MESH)
    for p in partner:
        pl.semaphore_signal(barrier, inc=1, device_id=(p, z), device_id_type=MESH)

    for c in loads[1:]:
        c.start()
    here.start()

    sent = []

    def remote(src, dst, to):
        n = len(sent)
        c = pltpu.make_async_remote_copy(
            src_ref=src, dst_ref=dst, send_sem=send.at[n], recv_sem=recv.at[n],
            device_id=(partner[to], z), device_id_type=MESH)
        sent.append(c)
        c.start()
        return c

    def transpose(src, dst):
        for h in range(heads):
            for n in range(chunks):
                dst[h, :, chunk(n)] = src[h, chunk(n)].T

    loads[0].wait()
    split_heads(flat.at[0], tmp, kh)
    transpose(kh, kt)
    loads[1].wait()
    split_heads(flat.at[1], tmp, vh)
    here.wait()

    pl.semaphore_wait(barrier, len(partner) + zs - 1)
    codes_sent = []
    for d in range(1, zs):
        c = pltpu.make_async_remote_copy(
            src_ref=codes_in.at[pl.ds(0, ROWS)], dst_ref=codes.at[z],
            send_sem=code_send.at[d - 1], recv_sem=code_recv.at[d - 1],
            device_id=(seq, lax.rem(z + d, zs)), device_id_type=MESH)
        c.start()
        codes_sent.append(c)

    @pl.loop(0, heads // 2)
    def _(pair):
        for i in range(2):
            h = 2 * pair + i
            for n in range(chunks):
                one[i, n] = dot(kt[h, :, chunk(n)], vh[h, chunk(n)])
            state[h] = total_of(one[i, n] for n in range(chunks))
            for m, (b, (lo, hi), _) in enumerate(PAIRS):
                acc = total_of(one[i, n] for n in range(lo, hi))
                states[m, h] = (acc * (scale * factor(8 + b))).astype(BF16)

    s_their = remote(state.at[pl.ds(theirs, 2)], r_state.at[pl.ds(theirs, 2)], 0)
    s_mine = remote(state.at[pl.ds(mine, 2)], r_state.at[pl.ds(mine, 2)], 0)

    def part(ref, s, *lead):
        return ref[(*lead, mine + s // SPLIT, pl.ds(s % SPLIT * half, half))]

    loads[3].wait()
    split_heads(flat.at[3], tmp, gh)
    transpose(gh, gt)

    s_their.wait_recv()
    up = [[]]
    for s in subs:
        tot[0, s] = part(state, s) + part(r_state, s)
        up[0].append(remote(tot.at[0, s], r_tot.at[0, s], 1))

    loads[2].wait()
    split_heads(flat.at[2], tmp, qh)
    transpose(qh, qt)

    def step_up(p, s):
        if s == 0:
            up.append([])
        up[p - 1][s].wait_recv()
        tot[p, s] = tot[p - 1, s] + r_tot[p - 1, s]
        up[p].append(remote(tot.at[p, s], r_tot.at[p, s], p + 1))

    def code_rows():
        for m in range(INNER + CROSS):
            for c in range(chunks):
                line = codes[c, 8 + m : 9 + m, :].astype(F32)
                lam[m, :, chunk(c)] = jnp.broadcast_to(line, (16, CHUNK)).astype(BF16)

    def by_code(m, matrix, rows):
        tiles = matrix.reshape(matrix.shape[0] // 16, 16, matrix.shape[1])
        return (tiles * lam[m, :, rows][None]).reshape(matrix.shape)

    def level_grads(bits, h):
        result = None
        for n in range(0, chunks, 2):
            rows = chunk(n, 2)
            query = qt[h, :, rows]
            tall = jnp.concatenate([by_code(INNER + b, query, rows) for b in bits], axis=0)
            found = dot(tall, gh[h, rows])
            result = found if result is None else result + found
        for i, b in enumerate(bits):
            level[b, h] = (scale * factor(11 + b) * on_bit(seq, b)) * result[
                i * CHUNK : (i + 1) * CHUNK]

    halves = [None] * CROSS

    def send_half(b):
        halves[b] = remote(
            level.at[b, pl.ds(theirs, 2)], r_level.at[b - 1, pl.ds(theirs, 2)], 0)

    for c in codes_sent:
        c.wait_recv()
    code_rows()
    for i in range(2):
        level_grads(range(CROSS), theirs + i)
    for b in (4, 3, 2, 1):
        send_half(b)
    for i in range(2):
        level_grads(range(CROSS), mine + i)
    whole = remote(level.at[0], r_level0, 0)
    for s in subs:
        step_up(1, s)
    halves[4].wait_recv()
    now = []
    for s in subs:
        down[0, s] = part(level, s, 4) + part(r_level, s, 3)
        now.append(remote(down.at[0, s], r_down.at[0, s], 4))
    def masks():
        s_at = lax.broadcasted_iota(jnp.int32, (CHUNK, CHUNK), 0)
        t_at = lax.broadcasted_iota(jnp.int32, (CHUNK, CHUNK), 1)
        differ = jnp.bitwise_xor(s_at, t_at)

        @pl.loop(0, chunks)
        def _(n):
            full = jnp.zeros((CHUNK, CHUNK), F32)
            for m in range(8):
                line = codes[n, m : m + 1, :].astype(F32) * (factor(m) * scale)
                if m == 0:
                    full = jnp.broadcast_to(line, (CHUNK, CHUNK))
                else:
                    full = jnp.where(differ >= 1 << (m - 1), line, full)
            mask[n] = jnp.where(s_at <= t_at, full, 0.0)

    def inner_grads(first):
        for h in range(first, first + 2):
            found = []
            for b, _, (lo, hi) in PAIRS:
                rows = chunk(lo, hi - lo)
                tall = by_code(b, qt[h, :, rows], rows)
                found.append((scale * factor(8 + b)) * dot(tall, gh[h, rows]))
            for n in range(chunks - 1):
                acc = total_of(
                    found[m] for m, (_, (lo, hi), _) in enumerate(PAIRS) if lo <= n < hi)
                value = acc.astype(BF16)
                inner[n, h] = value
                inner_t[n, h] = value.T

    def first_stage(u):
        h, start = u // 2, u % 2 * 4
        for i in range(4):
            rows = chunk(start + i)
            weights = mask[start + i]
            weight[u % 2, i, 0] = (weights * dot(vh[h, rows], gt[h, :, rows])).astype(BF16)
            weight[u % 2, i, 1] = (weights * dot(kh[h, rows], qt[h, :, rows])).astype(BF16)

    def second_stage(u):
        h, start = u // 2, u % 2 * 4
        for i in range(4):
            n = start + i
            rows = chunk(n)
            query, key, value, grad = qh[h, rows], kh[h, rows], vh[h, rows], gh[h, rows]
            weight_q, weight_v = weight[u % 2, i, 0], weight[u % 2, i, 1]
            if n < chunks - 1:
                dk[h, rows] = dot(
                    jnp.concatenate([weight_q, value], axis=1),
                    jnp.concatenate([query, inner_t[n, h]], axis=0))
                dv[h, rows] = dot(
                    jnp.concatenate([weight_v, key], axis=1),
                    jnp.concatenate([grad, inner[n, h]], axis=0))
            else:
                dk[h, rows] = dot(weight_q, query)
                dv[h, rows] = dot(weight_v, grad)
            left, right = [kt[h, :, rows]], [weight_q]
            for m, (b, _, (lo, hi)) in enumerate(PAIRS):
                if lo <= n < hi:
                    left.append(states[m, h])
                    right.append(by_code(b, gt[h, :, rows], rows))
            dq[h, :, rows] = dot(jnp.concatenate(left, axis=1), jnp.concatenate(right, axis=0))

    def diagonal(u):
        if u > 0:
            second_stage(u - 1)
        if u < 8:
            first_stage(u)

    def across(h):
        matrix = jnp.concatenate([cross[b, h] for b in range(CROSS)], axis=1)
        for n in range(0, chunks, 2):
            rows = chunk(n, 2)
            grad = gt[h, :, rows]
            tall = jnp.concatenate([by_code(INNER + b, grad, rows) for b in range(CROSS)], axis=0)
            result = (dq[h, :, rows] + dot(matrix, tall)).astype(BF16)
            for i in range(2):
                at = pl.ds((n + i) * CHUNK * heads + h, CHUNK, stride=heads)
                flat_q[at, :] = result[:, i * CHUNK : (i + 1) * CHUNK].T.astype(F32)

    def finish(h):
        at = pl.ds(h, count, stride=heads)
        matrix, zero = ks[h], jnp.zeros((CHUNK, CHUNK), BF16)
        both = jnp.concatenate([
            jnp.concatenate([matrix.T, zero], axis=1),
            jnp.concatenate([zero, matrix], axis=1)], axis=0)
        result = dot(jnp.concatenate([vh[h], kh[h]], axis=1), both)
        flat_k[at, :] = dk[h] + result[:, :CHUNK]
        flat_v[at, :] = dv[h] + result[:, CHUNK:]

    work = [masks, functools.partial(inner_grads, 0), functools.partial(inner_grads, 2)]
    work += [functools.partial(diagonal, u) for u in range(9)]

    def do(number=1):
        for _ in range(number):
            if work:
                work.pop(0)()

    do(3)
    found = []
    for n, b in enumerate((3, 2, 1)):
        halves[b].wait_recv()
        after = []
        for s in subs:
            now[s].wait_recv()
            value = r_down[n, s]
            if n:
                value = value + mid[n - 1, s]
            mid[n, s] = value
            down[n + 1, s] = value + part(level, s, b) + part(r_level, s, b - 1)
            after.append(remote(down.at[n + 1, s], r_down.at[n + 1, s], b))
            if n < 2:
                step_up(n + 2, s)
            else:
                up[3][s].wait_recv()
            if SPLIT == 2 or s % 2:
                do()
        now = after
        if n == 0:
            found.append(remote(r_tot.at[0], r_found.at[0], 0))
        found.append(remote(r_tot.at[n + 1], r_found.at[n + 1], 0))
    do(len(work))

    def cross_states(p):
        found[p].wait_recv()
        value = (scale * factor(12 + p)) * on_bit(seq, p + 1)
        for s in subs:
            rows = pl.ds(s % SPLIT * half, half)
            cross[p + 1, mine + s // SPLIT, rows] = (value * r_tot[p, s]).astype(BF16)
            cross[p + 1, theirs + s // SPLIT, rows] = (value * r_found[p, s]).astype(BF16)

    s_mine.wait_recv()
    for h in range(heads):
        cross[0, h] = ((scale * factor(11)) * on_bit(seq, 0) * r_state[h]).astype(BF16)
    for p in range(3):
        cross_states(p)
    last = []
    whole.wait_recv()
    for s in subs:
        now[s].wait_recv()
        mid[3, s] = mid[2, s] + r_down[3, s]
        last.append(remote(mid.at[3, s], r_mid.at[s], 0))
        rows = pl.ds(s % SPLIT * half, half)
        ks[mine + s // SPLIT, rows] = (mid[3, s] + part(r_level0, s)).astype(BF16)
        if s == 0:
            cross_states(3)
        if s % SPLIT == SPLIT - 1:
            across(2 * (s // SPLIT))
            across(2 * (s // SPLIT) + 1)
    for i in range(2):
        finish(mine + i)
    for s in subs:
        last[s].wait_recv()
        rows = pl.ds(s % SPLIT * half, half)
        ks[theirs + s // SPLIT, rows] = (r_mid[s] + r_level0[theirs + s // SPLIT, rows]).astype(BF16)
    for i in range(2):
        finish(theirs + i)

    for c in sent + codes_sent:
        c.wait_send()


def exchange(scale, zs, heads, q, k, v, g, codes):
    count, width = q.shape[0] // heads, q.shape[1]
    chunks = count // CHUNK
    square = (width, width)
    piece = (4, 2 * SPLIT, CHUNK // SPLIT, width)
    hbm = pl.BlockSpec(memory_space=pltpu.HBM)
    vmem = pl.BlockSpec(memory_space=pltpu.VMEM)
    messages = 2 + 4 + 4 + 1 + 18 * SPLIT
    flat = jax.ShapeDtypeStruct((heads * count, width), F32)
    return pl.pallas_call(
        functools.partial(exchange_kernel, scale, zs),
        out_shape=(flat,) * 3,
        in_specs=[hbm] * 5,
        out_specs=(vmem,) * 3,
        scratch_shapes=[
            pltpu.VMEM((4, heads * count, width), BF16),
            pltpu.VMEM((heads * count, width), F32),
            *[pltpu.VMEM((heads, count, width), BF16)] * 4,
            *[pltpu.VMEM((heads, width, count), BF16)] * 3,
            pltpu.VMEM((INNER + CROSS, 16, count), BF16),
            pltpu.VMEM((zs, ROWS, CHUNK), jnp.int32),
            pltpu.VMEM((2, chunks, *square), F32),
            pltpu.VMEM((len(PAIRS), heads, *square), BF16),
            *[pltpu.VMEM((chunks - 1, heads, *square), BF16)] * 2,
            pltpu.VMEM((chunks, CHUNK, CHUNK), F32),
            pltpu.VMEM((2, 4, 2, CHUNK, CHUNK), BF16),
            pltpu.VMEM((heads, width, count), F32),
            *[pltpu.VMEM((heads, count, width), F32)] * 2,
            pltpu.VMEM((CROSS, heads, *square), BF16),
            pltpu.VMEM((heads, *square), BF16),
            pltpu.VMEM((heads, *square), F32),
            pltpu.VMEM((heads, *square), F32),
            *[pltpu.VMEM(piece, F32)] * 3,
            pltpu.VMEM((CROSS, heads, *square), F32),
            pltpu.VMEM((4, heads, *square), F32),
            pltpu.VMEM((heads, *square), F32),
            *[pltpu.VMEM(piece, F32)] * 3,
            pltpu.VMEM(piece[1:], F32),
            pltpu.SemaphoreType.DMA((5,)),
            pltpu.SemaphoreType.DMA((zs - 1,)),
            pltpu.SemaphoreType.DMA((zs - 1,)),
            pltpu.SemaphoreType.DMA((messages,)),
            pltpu.SemaphoreType.DMA((messages,)),
        ],
        compiler_params=pltpu.CompilerParams(
            collective_id=0, has_side_effects=True, vmem_limit_bytes=LIMIT),
        name="exchange",
    )(q, k, v, g, codes)


LIMIT = 44 << 20


def pack_kernel(q_in, k_in, v_in, q_out, k_out, v_out, stage, sem):
    rows = q_in.shape[0] // 4
    copies = []
    for i, (src, dst) in enumerate(((q_in, q_out), (k_in, k_out), (v_in, v_out))):
        for n in range(4):
            at = pl.ds(n * rows, rows)
            stage[i, at] = src[at, :].astype(BF16)
            c = pltpu.make_async_copy(stage.at[i, at], dst.at[at], sem.at[i, n])
            c.start()
            copies.append(c)
    for c in copies:
        c.wait()


def pack(*flat):
    shape = flat[0].shape
    return pl.pallas_call(
        pack_kernel,
        out_shape=(jax.ShapeDtypeStruct(shape, BF16),) * 3,
        in_specs=[pl.BlockSpec(memory_space=pltpu.VMEM)] * 3,
        out_specs=(pl.BlockSpec(memory_space=pltpu.HBM),) * 3,
        scratch_shapes=[pltpu.VMEM((3, *shape), BF16), pltpu.SemaphoreType.DMA((3, 4))],
        compiler_params=pltpu.CompilerParams(vmem_limit_bytes=16 << 20),
        name="pack",
    )(*flat)


def on_device(queries, keys, values, out_grad, level_codes):
    count, heads, width = queries.shape
    scale = width ** (-0.5)
    flat = [x.reshape(count * heads, width) for x in (queries, keys, values, out_grad)]
    *flat, codes = [
        pltpu.with_memory_space_constraint(x, pltpu.HBM) for x in (*flat, level_codes)]
    grads = pack(*exchange(scale, lax.axis_size("head"), heads, *flat, codes))
    return tuple(x.reshape(count, heads, width) for x in grads)


def solution(mesh):
    return jax.shard_map(
        on_device,
        mesh=mesh,
        in_specs=(
            P("seq", "head", None),
            P("seq", "head", None),
            P("seq", "head", None),
            P("seq", "head", None),
            P(None, ("seq", "head")),
        ),
        out_specs=(P("seq", "head", None), P("seq", "head", None), P("seq", "head", None)),
        check_vma=False,
    )
```

```python
import functools

import jax
import jax.numpy as jnp
from jax import lax
from jax.experimental import pallas as pl
from jax.experimental.pallas import tpu as pltpu
from jax.sharding import PartitionSpec as P

MESH = pl.DeviceIdType.MESH
F32 = jnp.float32
BF16 = jnp.bfloat16
CHUNK = 128
INNER = 3
CROSS = 5
ROWS = 16
SPLIT = 2
SOONER = 4
PARTNERS = (1, 2, 6, 8, 24)

NN = (((1,), (0,)), ((), ()))
NT = (((1,), (1,)), ((), ()))
TN = (((0,), (0,)), ((), ()))


def dot(a, b, dims=NN):
    return lax.dot_general(a, b, dims, preferred_element_type=F32)


def factor(level):
    return 2.0 ** (-0.5 * max(level - 1, 0)) / 16.0


def on_bit(index, bit):
    return lax.rem(jnp.right_shift(index, bit), 2).astype(F32)


def split_heads(flat, tmp, out):
    heads, count, _ = out.shape
    tmp[...] = flat[...].astype(F32)
    for h in range(heads):
        out[h] = tmp[pl.ds(h, count, stride=heads), :].astype(BF16)


def far_first(zs):
    return sorted(range(1, zs), key=lambda d: -min(d, zs - d))


def chunk(n, count=1):
    return pl.ds(n * CHUNK, count * CHUNK)


def total_of(items):
    items = list(items)
    acc = items[0]
    for x in items[1:]:
        acc = acc + x
    return acc


PAIRS = (
    (0, (0, 1), (1, 2)), (0, (2, 3), (3, 4)), (0, (4, 5), (5, 6)), (0, (6, 7), (7, 8)),
    (1, (0, 2), (2, 4)), (1, (4, 6), (6, 8)),
    (2, (0, 4), (4, 8)),
)


def exchange_kernel(
    scale, zs,
    q_in, k_in, v_in, g_in, codes_in,
    out_q, flat_k, flat_v,
    flat, tmp, qh, kh, vh, gh, qt, kt, gt, lam, codes,
    one, states, inner, inner_t, mask, weight, dq, dk, dv, cross, ks,
    state, r_state, tot, r_tot, r_found,
    level, r_level, r_level0, down, r_down, mid, r_mid,
    in_sem, code_send, code_recv, send, recv,
):
    seq = lax.axis_index("seq")
    z = lax.axis_index("head")
    mine = 2 * lax.rem(seq, 2)
    theirs = 2 - mine
    heads, count, width = qh.shape
    chunks = count // CHUNK
    subs = range(2 * SPLIT)
    half = CHUNK // SPLIT
    partner = [jnp.bitwise_xor(seq, p) for p in PARTNERS]

    loads = [
        pltpu.make_async_copy(src, flat.at[i], in_sem.at[i])
        for i, src in enumerate((k_in, v_in, q_in, g_in))
    ]
    here = pltpu.make_async_copy(codes_in.at[pl.ds(0, ROWS)], codes.at[z], in_sem.at[4])
    loads[0].start()
    barrier = pltpu.get_barrier_semaphore()
    for d in far_first(zs):
        pl.semaphore_signal(
            barrier, inc=1, device_id=(seq, lax.rem(z + d, zs)), device_id_type=MESH)
    for p in partner:
        pl.semaphore_signal(barrier, inc=1, device_id=(p, z), device_id_type=MESH)

    for c in loads[1:]:
        c.start()
    here.start()
    codes_sent = [
        pltpu.make_async_remote_copy(
            src_ref=codes_in.at[pl.ds(0, ROWS)], dst_ref=codes.at[z],
            send_sem=code_send.at[d - 1], recv_sem=code_recv.at[d - 1],
            device_id=(seq, lax.rem(z + d, zs)), device_id_type=MESH)
        for d in far_first(zs)
    ]

    def enter():
        pl.semaphore_wait(barrier, len(partner) + zs - 1)
        for c in codes_sent:
            c.start()

    pl.when(z >= SOONER)(enter)

    sent = []

    def remote(src, dst, to):
        n = len(sent)
        c = pltpu.make_async_remote_copy(
            src_ref=src, dst_ref=dst, send_sem=send.at[n], recv_sem=recv.at[n],
            device_id=(partner[to], z), device_id_type=MESH)
        sent.append(c)
        c.start()
        return c

    def transpose(src, dst):
        for h in range(heads):
            for n in range(chunks):
                dst[h, :, chunk(n)] = src[h, chunk(n)].T

    loads[0].wait()
    split_heads(flat.at[0], tmp, kh)
    transpose(kh, kt)
    loads[1].wait()
    split_heads(flat.at[1], tmp, vh)
    here.wait()

    @pl.loop(0, heads // 2)
    def _(pair):
        for i in range(2):
            h = 2 * pair + i
            for n in range(chunks):
                one[i, n] = dot(kt[h, :, chunk(n)], vh[h, chunk(n)])
            state[h] = total_of(one[i, n] for n in range(chunks))
            for m, (b, (lo, hi), _) in enumerate(PAIRS):
                acc = total_of(one[i, n] for n in range(lo, hi))
                states[m, h] = (acc * (scale * factor(8 + b))).astype(BF16)

    loads[3].wait()
    split_heads(flat.at[3], tmp, gh)
    transpose(gh, gt)

    loads[2].wait()
    split_heads(flat.at[2], tmp, qh)
    transpose(qh, qt)

    pl.when(z < SOONER)(enter)
    s_their = remote(state.at[pl.ds(theirs, 2)], r_state.at[pl.ds(theirs, 2)], 0)
    s_mine = remote(state.at[pl.ds(mine, 2)], r_state.at[pl.ds(mine, 2)], 0)

    def part(ref, s, *lead):
        return ref[(*lead, mine + s // SPLIT, pl.ds(s % SPLIT * half, half))]

    s_their.wait_recv()
    up = [[]]
    for s in subs:
        tot[0, s] = part(state, s) + part(r_state, s)

    def step_up(p, s):
        if s == 0:
            up.append([])
        up[p - 1][s].wait_recv()
        tot[p, s] = tot[p - 1, s] + r_tot[p - 1, s]
        up[p].append(remote(tot.at[p, s], r_tot.at[p, s], p + 1))

    def code_rows(first, number):
        for m in range(first, first + number):
            for c in range(chunks):
                line = codes[c, 8 + m : 9 + m, :].astype(F32)
                lam[m, :, chunk(c)] = jnp.broadcast_to(line, (16, CHUNK)).astype(BF16)

    def by_code(m, matrix, rows):
        tiles = matrix.reshape(matrix.shape[0] // 16, 16, matrix.shape[1])
        return (tiles * lam[m, :, rows][None]).reshape(matrix.shape)

    def level_grads(bits, h):
        result = None
        for n in range(0, chunks, 2):
            rows = chunk(n, 2)
            query = qt[h, :, rows]
            tall = jnp.concatenate([by_code(INNER + b, query, rows) for b in bits], axis=0)
            found = dot(tall, gh[h, rows])
            result = found if result is None else result + found
        for i, b in enumerate(bits):
            level[b, h] = (scale * factor(11 + b) * on_bit(seq, b)) * result[
                i * CHUNK : (i + 1) * CHUNK]

    halves = [None] * CROSS

    def send_half(b):
        halves[b] = remote(
            level.at[b, pl.ds(theirs, 2)], r_level.at[b - 1, pl.ds(theirs, 2)], 0)

    for c in codes_sent:
        c.wait_recv()
    code_rows(INNER + 4, 1)
    for i in range(2):
        level_grads((4,), theirs + i)
    send_half(4)
    for i in range(2):
        level_grads((4,), mine + i)
    code_rows(0, INNER + 4)
    for i in range(2):
        level_grads(range(4), theirs + i)
    for b in (3, 2, 1):
        send_half(b)
    halves[4].wait_recv()
    now = []
    for s in subs:
        down[0, s] = part(level, s, 4) + part(r_level, s, 3)
        now.append(remote(down.at[0, s], r_down.at[0, s], 4))
        up[0].append(remote(tot.at[0, s], r_tot.at[0, s], 1))
    for i in range(2):
        level_grads(range(4), mine + i)
    whole = remote(level.at[0], r_level0, 0)

    def masks():
        s_at = lax.broadcasted_iota(jnp.int32, (CHUNK, CHUNK), 0)
        t_at = lax.broadcasted_iota(jnp.int32, (CHUNK, CHUNK), 1)
        differ = jnp.bitwise_xor(s_at, t_at)

        @pl.loop(0, chunks)
        def _(n):
            full = jnp.zeros((CHUNK, CHUNK), F32)
            for m in range(8):
                line = codes[n, m : m + 1, :].astype(F32) * (factor(m) * scale)
                if m == 0:
                    full = jnp.broadcast_to(line, (CHUNK, CHUNK))
                else:
                    full = jnp.where(differ >= 1 << (m - 1), line, full)
            mask[n] = jnp.where(s_at <= t_at, full, 0.0)

    def inner_grads(first):
        for h in range(first, first + 2):
            found = []
            for b, _, (lo, hi) in PAIRS:
                rows = chunk(lo, hi - lo)
                tall = by_code(b, qt[h, :, rows], rows)
                found.append((scale * factor(8 + b)) * dot(tall, gh[h, rows]))
            for n in range(chunks - 1):
                acc = total_of(
                    found[m] for m, (_, (lo, hi), _) in enumerate(PAIRS) if lo <= n < hi)
                value = acc.astype(BF16)
                inner[n, h] = value
                inner_t[n, h] = value.T

    def first_stage(u):
        h, start = u // 2, u % 2 * 4
        for i in range(4):
            rows = chunk(start + i)
            weights = mask[start + i]
            weight[u % 2, i, 0] = (weights * dot(vh[h, rows], gt[h, :, rows])).astype(BF16)
            weight[u % 2, i, 1] = (weights * dot(kh[h, rows], qt[h, :, rows])).astype(BF16)

    def second_stage(u):
        h, start = u // 2, u % 2 * 4
        for i in range(4):
            n = start + i
            rows = chunk(n)
            query, key, value, grad = qh[h, rows], kh[h, rows], vh[h, rows], gh[h, rows]
            weight_q, weight_v = weight[u % 2, i, 0], weight[u % 2, i, 1]
            if n < chunks - 1:
                dk[h, rows] = dot(
                    jnp.concatenate([weight_q, value], axis=1),
                    jnp.concatenate([query, inner_t[n, h]], axis=0))
                dv[h, rows] = dot(
                    jnp.concatenate([weight_v, key], axis=1),
                    jnp.concatenate([grad, inner[n, h]], axis=0))
            else:
                dk[h, rows] = dot(weight_q, query)
                dv[h, rows] = dot(weight_v, grad)
            left, right = [kt[h, :, rows]], [weight_q]
            for m, (b, _, (lo, hi)) in enumerate(PAIRS):
                if lo <= n < hi:
                    left.append(states[m, h])
                    right.append(by_code(b, gt[h, :, rows], rows))
            dq[h, :, rows] = dot(jnp.concatenate(left, axis=1), jnp.concatenate(right, axis=0))

    def diagonal(u):
        if u > 0:
            second_stage(u - 1)
        if u < 8:
            first_stage(u)

    def across(h):
        matrix = jnp.concatenate([cross[b, h] for b in range(4)], axis=1)
        for n in range(0, chunks, 2):
            rows = chunk(n, 2)
            grad = gt[h, :, rows]
            tall = jnp.concatenate([by_code(INNER + b, grad, rows) for b in range(4)], axis=0)
            dq[h, :, rows] += dot(matrix, tall)

    def across_last(h):
        for n in range(0, chunks, 2):
            rows = chunk(n, 2)
            extra = dot(cross[4, h], by_code(INNER + 4, gt[h, :, rows], rows))
            result = (dq[h, :, rows] + extra).astype(BF16)
            for i in range(2):
                at = pl.ds((n + i) * CHUNK * heads + h, CHUNK, stride=heads)
                tmp[at, :] = result[:, i * CHUNK : (i + 1) * CHUNK].T.astype(F32)

    def finish(h):
        at = pl.ds(h, count, stride=heads)
        matrix, zero = ks[h], jnp.zeros((CHUNK, CHUNK), BF16)
        both = jnp.concatenate([
            jnp.concatenate([matrix.T, zero], axis=1),
            jnp.concatenate([zero, matrix], axis=1)], axis=0)
        result = dot(jnp.concatenate([vh[h], kh[h]], axis=1), both)
        flat_k[at, :] = dk[h] + result[:, :CHUNK]
        flat_v[at, :] = dv[h] + result[:, CHUNK:]

    work = [masks, functools.partial(inner_grads, 0), functools.partial(inner_grads, 2)]
    work += [functools.partial(diagonal, u) for u in range(9)]

    def do(number=1):
        for _ in range(number):
            if work:
                work.pop(0)()

    do(3)
    found = []
    for n, b in enumerate((3, 2, 1)):
        halves[b].wait_recv()
        after = []
        for s in subs:
            now[s].wait_recv()
            value = r_down[n, s]
            if n:
                value = value + mid[n - 1, s]
            mid[n, s] = value
            down[n + 1, s] = value + part(level, s, b) + part(r_level, s, b - 1)
            after.append(remote(down.at[n + 1, s], r_down.at[n + 1, s], b))
            step_up(n + 1, s)
            if SPLIT == 2 or s % 2:
                do()
        now = after
        found.append(remote(r_tot.at[n], r_found.at[n], 0))
    do(len(work))

    def cross_states(p, ref, first):
        value = (scale * factor(12 + p)) * on_bit(seq, p + 1)
        for s in subs:
            rows = pl.ds(s % SPLIT * half, half)
            cross[p + 1, first + s // SPLIT, rows] = (value * ref[p, s]).astype(BF16)

    s_mine.wait_recv()
    for h in range(heads):
        cross[0, h] = ((scale * factor(11)) * on_bit(seq, 0) * r_state[h]).astype(BF16)
    for p in range(3):
        cross_states(p, r_tot, mine)
        found[p].wait_recv()
        cross_states(p, r_found, theirs)
    for h in range(heads):
        across(h)
    last = []
    whole.wait_recv()
    for s in subs:
        now[s].wait_recv()
        mid[3, s] = mid[2, s] + r_down[3, s]
        last.append(remote(mid.at[3, s], r_mid.at[s], 0))
        rows = pl.ds(s % SPLIT * half, half)
        ks[mine + s // SPLIT, rows] = (mid[3, s] + part(r_level0, s)).astype(BF16)
        up[3][s].wait_recv()
    found.append(remote(r_tot.at[3], r_found.at[3], 0))
    cross_states(3, r_tot, mine)
    for i in range(2):
        finish(mine + i)
        across_last(mine + i)
    for s in subs:
        last[s].wait_recv()
        rows = pl.ds(s % SPLIT * half, half)
        ks[theirs + s // SPLIT, rows] = (r_mid[s] + r_level0[theirs + s // SPLIT, rows]).astype(BF16)
    found[3].wait_recv()
    cross_states(3, r_found, theirs)
    for i in range(2):
        finish(theirs + i)
        across_last(theirs + i)
    out_q[...] = tmp[...].astype(BF16)

    for c in sent + codes_sent:
        c.wait_send()


def exchange(scale, zs, heads, q, k, v, g, codes):
    count, width = q.shape[0] // heads, q.shape[1]
    chunks = count // CHUNK
    square = (width, width)
    piece = (4, 2 * SPLIT, CHUNK // SPLIT, width)
    hbm = pl.BlockSpec(memory_space=pltpu.HBM)
    vmem = pl.BlockSpec(memory_space=pltpu.VMEM)
    messages = 2 + 4 + 4 + 1 + 18 * SPLIT
    flat = jax.ShapeDtypeStruct((heads * count, width), F32)
    return pl.pallas_call(
        functools.partial(exchange_kernel, scale, zs),
        out_shape=(jax.ShapeDtypeStruct(flat.shape, BF16), flat, flat),
        in_specs=[hbm] * 5,
        out_specs=(vmem,) * 3,
        scratch_shapes=[
            pltpu.VMEM((4, heads * count, width), BF16),
            pltpu.VMEM((heads * count, width), F32),
            *[pltpu.VMEM((heads, count, width), BF16)] * 4,
            *[pltpu.VMEM((heads, width, count), BF16)] * 3,
            pltpu.VMEM((INNER + CROSS, 16, count), BF16),
            pltpu.VMEM((zs, ROWS, CHUNK), jnp.int32),
            pltpu.VMEM((2, chunks, *square), F32),
            pltpu.VMEM((len(PAIRS), heads, *square), BF16),
            *[pltpu.VMEM((chunks - 1, heads, *square), BF16)] * 2,
            pltpu.VMEM((chunks, CHUNK, CHUNK), F32),
            pltpu.VMEM((2, 4, 2, CHUNK, CHUNK), BF16),
            pltpu.VMEM((heads, width, count), F32),
            *[pltpu.VMEM((heads, count, width), F32)] * 2,
            pltpu.VMEM((CROSS, heads, *square), BF16),
            pltpu.VMEM((heads, *square), BF16),
            pltpu.VMEM((heads, *square), F32),
            pltpu.VMEM((heads, *square), F32),
            *[pltpu.VMEM(piece, F32)] * 3,
            pltpu.VMEM((CROSS, heads, *square), F32),
            pltpu.VMEM((4, heads, *square), F32),
            pltpu.VMEM((heads, *square), F32),
            *[pltpu.VMEM(piece, F32)] * 3,
            pltpu.VMEM(piece[1:], F32),
            pltpu.SemaphoreType.DMA((5,)),
            pltpu.SemaphoreType.DMA((zs - 1,)),
            pltpu.SemaphoreType.DMA((zs - 1,)),
            pltpu.SemaphoreType.DMA((messages,)),
            pltpu.SemaphoreType.DMA((messages,)),
        ],
        compiler_params=pltpu.CompilerParams(
            collective_id=0, has_side_effects=True, vmem_limit_bytes=LIMIT),
        name="exchange",
    )(q, k, v, g, codes)


LIMIT = 44 << 20
PIECES = 4


def pack_kernel(q_in, k_in, v_in, q_out, k_out, v_out, stage, sem):
    rows = q_in.shape[0] // PIECES
    copies = [pltpu.make_async_copy(q_in, q_out, sem.at[2, 0])]
    copies[0].start()
    for n in range(PIECES):
        at = pl.ds(n * rows, rows)
        for i, (src, dst) in enumerate(((k_in, k_out), (v_in, v_out))):
            stage[i, at] = src[at, :].astype(BF16)
            c = pltpu.make_async_copy(stage.at[i, at], dst.at[at], sem.at[i, n])
            c.start()
            copies.append(c)
    for c in copies:
        c.wait()


def pack(*flat):
    shape = flat[0].shape
    return pl.pallas_call(
        pack_kernel,
        out_shape=(jax.ShapeDtypeStruct(shape, BF16),) * 3,
        in_specs=[pl.BlockSpec(memory_space=pltpu.VMEM)] * 3,
        out_specs=(pl.BlockSpec(memory_space=pltpu.HBM),) * 3,
        scratch_shapes=[pltpu.VMEM((2, *shape), BF16), pltpu.SemaphoreType.DMA((3, PIECES))],
        compiler_params=pltpu.CompilerParams(vmem_limit_bytes=16 << 20),
        name="pack",
    )(*flat)


def on_device(queries, keys, values, out_grad, level_codes):
    count, heads, width = queries.shape
    scale = width ** (-0.5)
    flat = [x.reshape(count * heads, width) for x in (queries, keys, values, out_grad)]
    *flat, codes = [
        pltpu.with_memory_space_constraint(x, pltpu.HBM) for x in (*flat, level_codes)]
    grads = pack(*exchange(scale, lax.axis_size("head"), heads, *flat, codes))
    return tuple(x.reshape(count, heads, width) for x in grads)


def solution(mesh):
    return jax.shard_map(
        on_device,
        mesh=mesh,
        in_specs=(
            P("seq", "head", None),
            P("seq", "head", None),
            P("seq", "head", None),
            P("seq", "head", None),
            P(None, ("seq", "head")),
        ),
        out_specs=(P("seq", "head", None), P("seq", "head", None), P("seq", "head", None)),
        check_vma=False,
    )
```

```python
import functools

import jax
import jax.numpy as jnp
from jax import lax
from jax.experimental import pallas as pl
from jax.experimental.pallas import tpu as pltpu
from jax.sharding import PartitionSpec as P

MESH = pl.DeviceIdType.MESH
F32 = jnp.float32
BF16 = jnp.bfloat16
CHUNK = 128
INNER = 3
CROSS = 5
ROWS = 16
SPLIT = 2
SOONER = 4
PARTNERS = (1, 2, 6, 8, 24)

NN = (((1,), (0,)), ((), ()))
NT = (((1,), (1,)), ((), ()))
TN = (((0,), (0,)), ((), ()))


def dot(a, b, dims=NN):
    return lax.dot_general(a, b, dims, preferred_element_type=F32)


def factor(level):
    return 2.0 ** (-0.5 * max(level - 1, 0)) / 16.0


def on_bit(index, bit):
    return lax.rem(jnp.right_shift(index, bit), 2).astype(F32)


def split_heads(flat, tmp, out):
    heads, count, _ = out.shape
    tmp[...] = flat[...].astype(F32)
    for h in range(heads):
        out[h] = tmp[pl.ds(h, count, stride=heads), :].astype(BF16)


def far_first(zs):
    return sorted(range(1, zs), key=lambda d: -min(d, zs - d))


def chunk(n, count=1):
    return pl.ds(n * CHUNK, count * CHUNK)


def total_of(items):
    items = list(items)
    acc = items[0]
    for x in items[1:]:
        acc = acc + x
    return acc


PAIRS = (
    (0, (0, 1), (1, 2)), (0, (2, 3), (3, 4)), (0, (4, 5), (5, 6)), (0, (6, 7), (7, 8)),
    (1, (0, 2), (2, 4)), (1, (4, 6), (6, 8)),
    (2, (0, 4), (4, 8)),
)


def exchange_kernel(
    scale, zs,
    q_in, k_in, v_in, g_in, codes_in,
    out_q, flat_k, flat_v,
    flat, tmp, qh, kh, vh, gh, qt, kt, gt, lam, codes,
    one, states, inner, inner_t, mask, weight, dq, dk, dv, cross, ks,
    state, r_state, tot, r_tot, r_found,
    level, r_level, r_level0, down, r_down, mid, r_mid,
    in_sem, code_send, code_recv, send, recv,
):
    seq = lax.axis_index("seq")
    z = lax.axis_index("head")
    mine = 2 * lax.rem(seq, 2)
    theirs = 2 - mine
    heads, count, width = qh.shape
    chunks = count // CHUNK
    subs = range(2 * SPLIT)
    half = CHUNK // SPLIT
    partner = [jnp.bitwise_xor(seq, p) for p in PARTNERS]

    loads = [
        pltpu.make_async_copy(src, flat.at[i], in_sem.at[i])
        for i, src in enumerate((k_in, v_in, q_in, g_in))
    ]
    here = pltpu.make_async_copy(codes_in.at[pl.ds(0, ROWS)], codes.at[z], in_sem.at[4])
    loads[0].start()
    barrier = pltpu.get_barrier_semaphore()
    for d in far_first(zs):
        pl.semaphore_signal(
            barrier, inc=1, device_id=(seq, lax.rem(z + d, zs)), device_id_type=MESH)
    for p in partner:
        pl.semaphore_signal(barrier, inc=1, device_id=(p, z), device_id_type=MESH)

    for c in loads[1:]:
        c.start()
    here.start()
    codes_sent = [
        pltpu.make_async_remote_copy(
            src_ref=codes_in.at[pl.ds(0, ROWS)], dst_ref=codes.at[z],
            send_sem=code_send.at[d - 1], recv_sem=code_recv.at[d - 1],
            device_id=(seq, lax.rem(z + d, zs)), device_id_type=MESH)
        for d in far_first(zs)
    ]

    def enter():
        pl.semaphore_wait(barrier, len(partner) + zs - 1)
        for c in codes_sent:
            c.start()

    pl.when(z >= SOONER)(enter)

    sent = []

    top = lax.rem(jnp.right_shift(seq, 4), 2)
    some = []

    def remote(src, dst, to, sends=None):
        n = len(sent)
        c = pltpu.make_async_remote_copy(
            src_ref=src, dst_ref=dst, send_sem=send.at[n], recv_sem=recv.at[n],
            device_id=(partner[to], z), device_id_type=MESH)
        sent.append(c)
        if sends is None:
            c.start()
        else:
            pl.when(sends)(c.start)
            some.append((n, sends))
        return c

    def transpose(src, dst):
        for h in range(heads):
            for n in range(chunks):
                dst[h, :, chunk(n)] = src[h, chunk(n)].T

    loads[0].wait()
    split_heads(flat.at[0], tmp, kh)
    transpose(kh, kt)
    loads[1].wait()
    split_heads(flat.at[1], tmp, vh)
    here.wait()

    @pl.loop(0, heads // 2)
    def _(pair):
        for i in range(2):
            h = 2 * pair + i
            for n in range(chunks):
                one[i, n] = dot(kt[h, :, chunk(n)], vh[h, chunk(n)])
            state[h] = total_of(one[i, n] for n in range(chunks))
            for m, (b, (lo, hi), _) in enumerate(PAIRS):
                acc = total_of(one[i, n] for n in range(lo, hi))
                states[m, h] = (acc * (scale * factor(8 + b))).astype(BF16)

    loads[3].wait()
    split_heads(flat.at[3], tmp, gh)
    transpose(gh, gt)

    loads[2].wait()
    split_heads(flat.at[2], tmp, qh)
    transpose(qh, qt)

    pl.when(z < SOONER)(enter)
    s_their = remote(state.at[pl.ds(theirs, 2)], r_state.at[pl.ds(theirs, 2)], 0)
    s_mine = remote(state.at[pl.ds(mine, 2)], r_state.at[pl.ds(mine, 2)], 0)

    def part(ref, s, *lead):
        return ref[(*lead, mine + s // SPLIT, pl.ds(s % SPLIT * half, half))]

    s_their.wait_recv()
    up = [[]]
    for s in subs:
        tot[0, s] = part(state, s) + part(r_state, s)

    def step_up(p, s):
        if s == 0:
            up.append([])
        up[p - 1][s].wait_recv()
        tot[p, s] = tot[p - 1, s] + r_tot[p - 1, s]
        up[p].append(
            remote(tot.at[p, s], r_tot.at[p, s], p + 1, None if p < 3 else top == 0))

    def code_rows(first, number):
        for m in range(first, first + number):
            for c in range(chunks):
                line = codes[c, 8 + m : 9 + m, :].astype(F32)
                lam[m, :, chunk(c)] = jnp.broadcast_to(line, (16, CHUNK)).astype(BF16)

    def by_code(m, matrix, rows):
        tiles = matrix.reshape(matrix.shape[0] // 16, 16, matrix.shape[1])
        return (tiles * lam[m, :, rows][None]).reshape(matrix.shape)

    def level_grads(bits, h):
        result = None
        for n in range(0, chunks, 2):
            rows = chunk(n, 2)
            query = qt[h, :, rows]
            tall = jnp.concatenate([by_code(INNER + b, query, rows) for b in bits], axis=0)
            found = dot(tall, gh[h, rows])
            result = found if result is None else result + found
        for i, b in enumerate(bits):
            level[b, h] = (scale * factor(11 + b) * on_bit(seq, b)) * result[
                i * CHUNK : (i + 1) * CHUNK]

    halves = [None] * CROSS

    def send_half(b):
        halves[b] = remote(
            level.at[b, pl.ds(theirs, 2)], r_level.at[b - 1, pl.ds(theirs, 2)], 0)

    for c in codes_sent:
        c.wait_recv()
    code_rows(INNER + 4, 1)
    for i in range(2):
        level_grads((4,), theirs + i)
    send_half(4)
    for i in range(2):
        level_grads((4,), mine + i)
    code_rows(0, INNER + 4)
    for i in range(2):
        level_grads(range(4), theirs + i)
    for b in (3, 2, 1):
        send_half(b)
    halves[4].wait_recv()
    now = []
    for s in subs:
        down[0, s] = part(level, s, 4) + part(r_level, s, 3)
        now.append(remote(down.at[0, s], r_down.at[0, s], 4, top == 1))
        up[0].append(remote(tot.at[0, s], r_tot.at[0, s], 1))
    for i in range(2):
        level_grads(range(4), mine + i)
    whole = remote(level.at[0], r_level0, 0)

    def masks():
        s_at = lax.broadcasted_iota(jnp.int32, (CHUNK, CHUNK), 0)
        t_at = lax.broadcasted_iota(jnp.int32, (CHUNK, CHUNK), 1)
        differ = jnp.bitwise_xor(s_at, t_at)

        @pl.loop(0, chunks)
        def _(n):
            full = jnp.zeros((CHUNK, CHUNK), F32)
            for m in range(8):
                line = codes[n, m : m + 1, :].astype(F32) * (factor(m) * scale)
                if m == 0:
                    full = jnp.broadcast_to(line, (CHUNK, CHUNK))
                else:
                    full = jnp.where(differ >= 1 << (m - 1), line, full)
            mask[n] = jnp.where(s_at <= t_at, full, 0.0)

    def inner_grads(first):
        for h in range(first, first + 2):
            found = []
            for b, _, (lo, hi) in PAIRS:
                rows = chunk(lo, hi - lo)
                tall = by_code(b, qt[h, :, rows], rows)
                found.append((scale * factor(8 + b)) * dot(tall, gh[h, rows]))
            for n in range(chunks - 1):
                acc = total_of(
                    found[m] for m, (_, (lo, hi), _) in enumerate(PAIRS) if lo <= n < hi)
                value = acc.astype(BF16)
                inner[n, h] = value
                inner_t[n, h] = value.T

    def first_stage(u):
        h, start = u // 2, u % 2 * 4
        for i in range(4):
            rows = chunk(start + i)
            weights = mask[start + i]
            weight[u % 2, i, 0] = (weights * dot(vh[h, rows], gt[h, :, rows])).astype(BF16)
            weight[u % 2, i, 1] = (weights * dot(kh[h, rows], qt[h, :, rows])).astype(BF16)

    def second_stage(u):
        h, start = u // 2, u % 2 * 4
        for i in range(4):
            n = start + i
            rows = chunk(n)
            query, key, value, grad = qh[h, rows], kh[h, rows], vh[h, rows], gh[h, rows]
            weight_q, weight_v = weight[u % 2, i, 0], weight[u % 2, i, 1]
            if n < chunks - 1:
                dk[h, rows] = dot(
                    jnp.concatenate([weight_q, value], axis=1),
                    jnp.concatenate([query, inner_t[n, h]], axis=0))
                dv[h, rows] = dot(
                    jnp.concatenate([weight_v, key], axis=1),
                    jnp.concatenate([grad, inner[n, h]], axis=0))
            else:
                dk[h, rows] = dot(weight_q, query)
                dv[h, rows] = dot(weight_v, grad)
            left, right = [kt[h, :, rows]], [weight_q]
            for m, (b, _, (lo, hi)) in enumerate(PAIRS):
                if lo <= n < hi:
                    left.append(states[m, h])
                    right.append(by_code(b, gt[h, :, rows], rows))
            dq[h, :, rows] = dot(jnp.concatenate(left, axis=1), jnp.concatenate(right, axis=0))

    def diagonal(u):
        if u > 0:
            second_stage(u - 1)
        if u < 8:
            first_stage(u)

    def across(h):
        matrix = jnp.concatenate([cross[b, h] for b in range(4)], axis=1)
        for n in range(0, chunks, 2):
            rows = chunk(n, 2)
            grad = gt[h, :, rows]
            tall = jnp.concatenate([by_code(INNER + b, grad, rows) for b in range(4)], axis=0)
            dq[h, :, rows] += dot(matrix, tall)

    def across_last(h):
        for n in range(0, chunks, 2):
            rows = chunk(n, 2)
            extra = dot(cross[4, h], by_code(INNER + 4, gt[h, :, rows], rows))
            result = (dq[h, :, rows] + extra).astype(BF16)
            for i in range(2):
                at = pl.ds((n + i) * CHUNK * heads + h, CHUNK, stride=heads)
                tmp[at, :] = result[:, i * CHUNK : (i + 1) * CHUNK].T.astype(F32)

    def finish(h):
        at = pl.ds(h, count, stride=heads)
        matrix, zero = ks[h], jnp.zeros((CHUNK, CHUNK), BF16)
        both = jnp.concatenate([
            jnp.concatenate([matrix.T, zero], axis=1),
            jnp.concatenate([zero, matrix], axis=1)], axis=0)
        result = dot(jnp.concatenate([vh[h], kh[h]], axis=1), both)
        flat_k[at, :] = dk[h] + result[:, :CHUNK]
        flat_v[at, :] = dv[h] + result[:, CHUNK:]

    work = [masks, functools.partial(inner_grads, 0), functools.partial(inner_grads, 2)]
    work += [functools.partial(diagonal, u) for u in range(9)]

    def do(number=1):
        for _ in range(number):
            if work:
                work.pop(0)()

    do(3)
    found = []
    for n, b in enumerate((3, 2, 1)):
        halves[b].wait_recv()
        after = []
        for s in subs:
            if n:
                now[s].wait_recv()
                value = r_down[n, s] + mid[n - 1, s]
            else:
                pl.when(top == 0)(now[s].wait_recv)
                value = jnp.where(top == 0, r_down[n, s], 0.0)
            mid[n, s] = value
            down[n + 1, s] = value + part(level, s, b) + part(r_level, s, b - 1)
            after.append(remote(down.at[n + 1, s], r_down.at[n + 1, s], b))
            step_up(n + 1, s)
            if SPLIT == 2 or s % 2:
                do()
        now = after
        found.append(remote(r_tot.at[n], r_found.at[n], 0))
    do(len(work))

    def cross_states(p, ref, first):
        value = scale * factor(12 + p)
        is_on = lax.rem(jnp.right_shift(seq, p + 1), 2) == 1
        for s in subs:
            rows = pl.ds(s % SPLIT * half, half)
            cross[p + 1, first + s // SPLIT, rows] = (
                jnp.where(is_on, value * ref[p, s], 0.0)).astype(BF16)

    s_mine.wait_recv()
    for h in range(heads):
        cross[0, h] = ((scale * factor(11)) * on_bit(seq, 0) * r_state[h]).astype(BF16)
    for p in range(3):
        cross_states(p, r_tot, mine)
        found[p].wait_recv()
        cross_states(p, r_found, theirs)
    for h in range(heads):
        across(h)
    last = []
    whole.wait_recv()
    for s in subs:
        now[s].wait_recv()
        mid[3, s] = mid[2, s] + r_down[3, s]
        last.append(remote(mid.at[3, s], r_mid.at[s], 0))
        rows = pl.ds(s % SPLIT * half, half)
        ks[mine + s // SPLIT, rows] = (mid[3, s] + part(r_level0, s)).astype(BF16)
        pl.when(top == 1)(up[3][s].wait_recv)
    found.append(remote(r_tot.at[3], r_found.at[3], 0, top == 1))
    cross_states(3, r_tot, mine)
    for i in range(2):
        finish(mine + i)
        across_last(mine + i)
    for s in subs:
        last[s].wait_recv()
        rows = pl.ds(s % SPLIT * half, half)
        ks[theirs + s // SPLIT, rows] = (r_mid[s] + r_level0[theirs + s // SPLIT, rows]).astype(BF16)
    pl.when(top == 1)(found[3].wait_recv)
    cross_states(3, r_found, theirs)
    for i in range(2):
        finish(theirs + i)
        across_last(theirs + i)
    out_q[...] = tmp[...].astype(BF16)

    rare = dict(some)
    for n, c in enumerate(sent):
        if n in rare:
            pl.when(rare[n])(c.wait_send)
        else:
            c.wait_send()
    for c in codes_sent:
        c.wait_send()


def exchange(scale, zs, heads, q, k, v, g, codes):
    count, width = q.shape[0] // heads, q.shape[1]
    chunks = count // CHUNK
    square = (width, width)
    piece = (4, 2 * SPLIT, CHUNK // SPLIT, width)
    hbm = pl.BlockSpec(memory_space=pltpu.HBM)
    vmem = pl.BlockSpec(memory_space=pltpu.VMEM)
    messages = 2 + 4 + 4 + 1 + 18 * SPLIT
    flat = jax.ShapeDtypeStruct((heads * count, width), F32)
    return pl.pallas_call(
        functools.partial(exchange_kernel, scale, zs),
        out_shape=(jax.ShapeDtypeStruct(flat.shape, BF16), flat, flat),
        in_specs=[hbm] * 5,
        out_specs=(vmem,) * 3,
        scratch_shapes=[
            pltpu.VMEM((4, heads * count, width), BF16),
            pltpu.VMEM((heads * count, width), F32),
            *[pltpu.VMEM((heads, count, width), BF16)] * 4,
            *[pltpu.VMEM((heads, width, count), BF16)] * 3,
            pltpu.VMEM((INNER + CROSS, 16, count), BF16),
            pltpu.VMEM((zs, ROWS, CHUNK), jnp.int32),
            pltpu.VMEM((2, chunks, *square), F32),
            pltpu.VMEM((len(PAIRS), heads, *square), BF16),
            *[pltpu.VMEM((chunks - 1, heads, *square), BF16)] * 2,
            pltpu.VMEM((chunks, CHUNK, CHUNK), F32),
            pltpu.VMEM((2, 4, 2, CHUNK, CHUNK), BF16),
            pltpu.VMEM((heads, width, count), F32),
            *[pltpu.VMEM((heads, count, width), F32)] * 2,
            pltpu.VMEM((CROSS, heads, *square), BF16),
            pltpu.VMEM((heads, *square), BF16),
            pltpu.VMEM((heads, *square), F32),
            pltpu.VMEM((heads, *square), F32),
            *[pltpu.VMEM(piece, F32)] * 3,
            pltpu.VMEM((CROSS, heads, *square), F32),
            pltpu.VMEM((4, heads, *square), F32),
            pltpu.VMEM((heads, *square), F32),
            *[pltpu.VMEM(piece, F32)] * 3,
            pltpu.VMEM(piece[1:], F32),
            pltpu.SemaphoreType.DMA((5,)),
            pltpu.SemaphoreType.DMA((zs - 1,)),
            pltpu.SemaphoreType.DMA((zs - 1,)),
            pltpu.SemaphoreType.DMA((messages,)),
            pltpu.SemaphoreType.DMA((messages,)),
        ],
        compiler_params=pltpu.CompilerParams(
            collective_id=0, has_side_effects=True, vmem_limit_bytes=LIMIT),
        name="exchange",
    )(q, k, v, g, codes)


LIMIT = 44 << 20
PIECES = 4


def pack_kernel(q_in, k_in, v_in, q_out, k_out, v_out, stage, sem):
    rows = q_in.shape[0] // PIECES
    copies = [pltpu.make_async_copy(q_in, q_out, sem.at[2, 0])]
    copies[0].start()
    for n in range(PIECES):
        at = pl.ds(n * rows, rows)
        for i, (src, dst) in enumerate(((k_in, k_out), (v_in, v_out))):
            stage[i, at] = src[at, :].astype(BF16)
            c = pltpu.make_async_copy(stage.at[i, at], dst.at[at], sem.at[i, n])
            c.start()
            copies.append(c)
    for c in copies:
        c.wait()


def pack(*flat):
    shape = flat[0].shape
    return pl.pallas_call(
        pack_kernel,
        out_shape=(jax.ShapeDtypeStruct(shape, BF16),) * 3,
        in_specs=[pl.BlockSpec(memory_space=pltpu.VMEM)] * 3,
        out_specs=(pl.BlockSpec(memory_space=pltpu.HBM),) * 3,
        scratch_shapes=[pltpu.VMEM((2, *shape), BF16), pltpu.SemaphoreType.DMA((3, PIECES))],
        compiler_params=pltpu.CompilerParams(vmem_limit_bytes=16 << 20),
        name="pack",
    )(*flat)


def on_device(queries, keys, values, out_grad, level_codes):
    count, heads, width = queries.shape
    scale = width ** (-0.5)
    flat = [x.reshape(count * heads, width) for x in (queries, keys, values, out_grad)]
    *flat, codes = [
        pltpu.with_memory_space_constraint(x, pltpu.HBM) for x in (*flat, level_codes)]
    grads = pack(*exchange(scale, lax.axis_size("head"), heads, *flat, codes))
    return tuple(x.reshape(count, heads, width) for x in grads)


def solution(mesh):
    return jax.shard_map(
        on_device,
        mesh=mesh,
        in_specs=(
            P("seq", "head", None),
            P("seq", "head", None),
            P("seq", "head", None),
            P("seq", "head", None),
            P(None, ("seq", "head")),
        ),
        out_specs=(P("seq", "head", None), P("seq", "head", None), P("seq", "head", None)),
        check_vma=False,
    )
```

```python
import functools

import jax
import jax.numpy as jnp
from jax import lax
from jax.experimental import pallas as pl
from jax.experimental.pallas import tpu as pltpu
from jax.sharding import PartitionSpec as P

MESH = pl.DeviceIdType.MESH
F32 = jnp.float32
BF16 = jnp.bfloat16
CHUNK = 128
INNER = 3
CROSS = 5
ROWS = 16
SPLIT = 2
SOONER = 4
PARTNERS = (1, 2, 6, 8, 24)

NN = (((1,), (0,)), ((), ()))
NT = (((1,), (1,)), ((), ()))
TN = (((0,), (0,)), ((), ()))


def dot(a, b, dims=NN):
    return lax.dot_general(a, b, dims, preferred_element_type=F32)


def factor(level):
    return 2.0 ** (-0.5 * max(level - 1, 0)) / 16.0


def on_bit(index, bit):
    return lax.rem(jnp.right_shift(index, bit), 2).astype(F32)


def split_heads(flat, tmp, out):
    heads, count, _ = out.shape
    tmp[...] = flat[...].astype(F32)
    for h in range(heads):
        out[h] = tmp[pl.ds(h, count, stride=heads), :].astype(BF16)


def far_first(zs):
    return sorted(range(1, zs), key=lambda d: -min(d, zs - d))


def chunk(n, count=1):
    return pl.ds(n * CHUNK, count * CHUNK)


def total_of(items):
    items = list(items)
    acc = items[0]
    for x in items[1:]:
        acc = acc + x
    return acc


PAIRS = (
    (0, (0, 1), (1, 2)), (0, (2, 3), (3, 4)), (0, (4, 5), (5, 6)), (0, (6, 7), (7, 8)),
    (1, (0, 2), (2, 4)), (1, (4, 6), (6, 8)),
    (2, (0, 4), (4, 8)),
)


def exchange_kernel(
    scale, zs,
    q_in, k_in, v_in, g_in, codes_in,
    out_q, flat_k, flat_v,
    flat, tmp, qh, kh, vh, gh, qt, kt, gt, lam, codes,
    one, states, inner, inner_t, mask, weight, dq, dk, dv, cross, ks,
    state, r_state, tot, r_tot, r_found,
    level, r_level, r_level0, down, r_down, mid, r_mid,
    in_sem, code_send, code_recv, send, recv,
):
    seq = lax.axis_index("seq")
    z = lax.axis_index("head")
    mine = 2 * lax.rem(seq, 2)
    theirs = 2 - mine
    heads, count, width = qh.shape
    chunks = count // CHUNK
    subs = range(2 * SPLIT)
    half = CHUNK // SPLIT
    partner = [jnp.bitwise_xor(seq, p) for p in PARTNERS]

    loads = [
        pltpu.make_async_copy(src, flat.at[i], in_sem.at[i])
        for i, src in enumerate((k_in, v_in, q_in, g_in))
    ]
    here = pltpu.make_async_copy(codes_in.at[pl.ds(0, ROWS)], codes.at[z], in_sem.at[4])
    loads[0].start()
    barrier = pltpu.get_barrier_semaphore()
    for d in far_first(zs):
        pl.semaphore_signal(
            barrier, inc=1, device_id=(seq, lax.rem(z + d, zs)), device_id_type=MESH)
    for p in partner:
        pl.semaphore_signal(barrier, inc=1, device_id=(p, z), device_id_type=MESH)

    for c in loads[1:]:
        c.start()
    here.start()
    codes_sent = [
        pltpu.make_async_remote_copy(
            src_ref=codes_in.at[pl.ds(0, ROWS)], dst_ref=codes.at[z],
            send_sem=code_send.at[d - 1], recv_sem=code_recv.at[d - 1],
            device_id=(seq, lax.rem(z + d, zs)), device_id_type=MESH)
        for d in far_first(zs)
    ]

    def enter():
        pl.semaphore_wait(barrier, len(partner) + zs - 1)
        for c in codes_sent:
            c.start()

    pl.when(z >= SOONER)(enter)

    sent = []

    top = lax.rem(jnp.right_shift(seq, 4), 2)
    some = []

    def remote(src, dst, to, sends=None):
        n = len(sent)
        c = pltpu.make_async_remote_copy(
            src_ref=src, dst_ref=dst, send_sem=send.at[n], recv_sem=recv.at[n],
            device_id=(partner[to], z), device_id_type=MESH)
        sent.append(c)
        if sends is None:
            c.start()
        else:
            pl.when(sends)(c.start)
            some.append((n, sends))
        return c

    def transpose(src, dst):
        for h in range(heads):
            for n in range(chunks):
                dst[h, :, chunk(n)] = src[h, chunk(n)].T

    loads[0].wait()
    split_heads(flat.at[0], tmp, kh)
    transpose(kh, kt)
    loads[1].wait()
    split_heads(flat.at[1], tmp, vh)
    here.wait()

    @pl.loop(0, heads // 2)
    def _(pair):
        for i in range(2):
            h = 2 * pair + i
            for n in range(chunks):
                one[i, n] = dot(kt[h, :, chunk(n)], vh[h, chunk(n)])
            state[h] = total_of(one[i, n] for n in range(chunks))
            for m, (b, (lo, hi), _) in enumerate(PAIRS):
                acc = total_of(one[i, n] for n in range(lo, hi))
                states[m, h] = (acc * (scale * factor(8 + b))).astype(BF16)

    loads[3].wait()
    split_heads(flat.at[3], tmp, gh)
    transpose(gh, gt)

    loads[2].wait()
    split_heads(flat.at[2], tmp, qh)
    transpose(qh, qt)

    pl.when(z < SOONER)(enter)
    s_their = remote(state.at[pl.ds(theirs, 2)], r_state.at[pl.ds(theirs, 2)], 0)
    s_mine = remote(state.at[pl.ds(mine, 2)], r_state.at[pl.ds(mine, 2)], 0, mine == 0)

    def part(ref, s, *lead):
        return ref[(*lead, mine + s // SPLIT, pl.ds(s % SPLIT * half, half))]

    s_their.wait_recv()
    up = [[]]
    for s in subs:
        tot[0, s] = part(state, s) + part(r_state, s)

    def step_up(p, s):
        if s == 0:
            up.append([])
        up[p - 1][s].wait_recv()
        tot[p, s] = tot[p - 1, s] + r_tot[p - 1, s]
        up[p].append(
            remote(tot.at[p, s], r_tot.at[p, s], p + 1, None if p < 3 else top == 0))

    def code_rows(first, number):
        for m in range(first, first + number):
            for c in range(chunks):
                line = codes[c, 8 + m : 9 + m, :].astype(F32)
                lam[m, :, chunk(c)] = jnp.broadcast_to(line, (16, CHUNK)).astype(BF16)

    def by_code(m, matrix, rows):
        tiles = matrix.reshape(matrix.shape[0] // 16, 16, matrix.shape[1])
        return (tiles * lam[m, :, rows][None]).reshape(matrix.shape)

    def level_grads(bits, h):
        result = None
        for n in range(0, chunks, 2):
            rows = chunk(n, 2)
            query = qt[h, :, rows]
            tall = jnp.concatenate([by_code(INNER + b, query, rows) for b in bits], axis=0)
            found = dot(tall, gh[h, rows])
            result = found if result is None else result + found
        for i, b in enumerate(bits):
            level[b, h] = (scale * factor(11 + b) * on_bit(seq, b)) * result[
                i * CHUNK : (i + 1) * CHUNK]

    halves = [None] * CROSS

    def send_half(b):
        halves[b] = remote(
            level.at[b, pl.ds(theirs, 2)], r_level.at[b - 1, pl.ds(theirs, 2)], 0)

    for c in codes_sent:
        c.wait_recv()
    code_rows(INNER + 4, 1)
    for i in range(2):
        level_grads((4,), theirs + i)
    send_half(4)
    for i in range(2):
        level_grads((4,), mine + i)
    code_rows(0, INNER + 4)
    for i in range(2):
        level_grads(range(4), theirs + i)
    for b in (3, 2, 1):
        send_half(b)
    halves[4].wait_recv()
    now = []
    for s in subs:
        down[0, s] = part(level, s, 4) + part(r_level, s, 3)
        now.append(remote(down.at[0, s], r_down.at[0, s], 4, top == 1))
        up[0].append(remote(tot.at[0, s], r_tot.at[0, s], 1))
    for i in range(2):
        level_grads(range(4), mine + i)
    whole = remote(level.at[0], r_level0, 0, mine != 0)

    def masks():
        s_at = lax.broadcasted_iota(jnp.int32, (CHUNK, CHUNK), 0)
        t_at = lax.broadcasted_iota(jnp.int32, (CHUNK, CHUNK), 1)
        differ = jnp.bitwise_xor(s_at, t_at)

        @pl.loop(0, chunks)
        def _(n):
            full = jnp.zeros((CHUNK, CHUNK), F32)
            for m in range(8):
                line = codes[n, m : m + 1, :].astype(F32) * (factor(m) * scale)
                if m == 0:
                    full = jnp.broadcast_to(line, (CHUNK, CHUNK))
                else:
                    full = jnp.where(differ >= 1 << (m - 1), line, full)
            mask[n] = jnp.where(s_at <= t_at, full, 0.0)

    def inner_grads(first):
        for h in range(first, first + 2):
            found = []
            for b, _, (lo, hi) in PAIRS:
                rows = chunk(lo, hi - lo)
                tall = by_code(b, qt[h, :, rows], rows)
                found.append((scale * factor(8 + b)) * dot(tall, gh[h, rows]))
            for n in range(chunks - 1):
                acc = total_of(
                    found[m] for m, (_, (lo, hi), _) in enumerate(PAIRS) if lo <= n < hi)
                value = acc.astype(BF16)
                inner[n, h] = value
                inner_t[n, h] = value.T

    def first_stage(u):
        h, start = u // 2, u % 2 * 4
        for i in range(4):
            rows = chunk(start + i)
            weights = mask[start + i]
            weight[u % 2, i, 0] = (weights * dot(vh[h, rows], gt[h, :, rows])).astype(BF16)
            weight[u % 2, i, 1] = (weights * dot(kh[h, rows], qt[h, :, rows])).astype(BF16)

    def second_stage(u):
        h, start = u // 2, u % 2 * 4
        for i in range(4):
            n = start + i
            rows = chunk(n)
            query, key, value, grad = qh[h, rows], kh[h, rows], vh[h, rows], gh[h, rows]
            weight_q, weight_v = weight[u % 2, i, 0], weight[u % 2, i, 1]
            if n < chunks - 1:
                dk[h, rows] = dot(
                    jnp.concatenate([weight_q, value], axis=1),
                    jnp.concatenate([query, inner_t[n, h]], axis=0))
                dv[h, rows] = dot(
                    jnp.concatenate([weight_v, key], axis=1),
                    jnp.concatenate([grad, inner[n, h]], axis=0))
            else:
                dk[h, rows] = dot(weight_q, query)
                dv[h, rows] = dot(weight_v, grad)
            left, right = [kt[h, :, rows]], [weight_q]
            for m, (b, _, (lo, hi)) in enumerate(PAIRS):
                if lo <= n < hi:
                    left.append(states[m, h])
                    right.append(by_code(b, gt[h, :, rows], rows))
            dq[h, :, rows] = dot(jnp.concatenate(left, axis=1), jnp.concatenate(right, axis=0))

    def diagonal(u):
        if u > 0:
            second_stage(u - 1)
        if u < 8:
            first_stage(u)

    def across(h):
        matrix = jnp.concatenate([cross[b, h] for b in range(4)], axis=1)
        for n in range(0, chunks, 2):
            rows = chunk(n, 2)
            grad = gt[h, :, rows]
            tall = jnp.concatenate([by_code(INNER + b, grad, rows) for b in range(4)], axis=0)
            dq[h, :, rows] += dot(matrix, tall)

    def across_last(h):
        for n in range(0, chunks, 2):
            rows = chunk(n, 2)
            extra = dot(cross[4, h], by_code(INNER + 4, gt[h, :, rows], rows))
            result = (dq[h, :, rows] + extra).astype(BF16)
            for i in range(2):
                at = pl.ds((n + i) * CHUNK * heads + h, CHUNK, stride=heads)
                tmp[at, :] = result[:, i * CHUNK : (i + 1) * CHUNK].T.astype(F32)

    def finish(h):
        at = pl.ds(h, count, stride=heads)
        matrix, zero = ks[h], jnp.zeros((CHUNK, CHUNK), BF16)
        both = jnp.concatenate([
            jnp.concatenate([matrix.T, zero], axis=1),
            jnp.concatenate([zero, matrix], axis=1)], axis=0)
        result = dot(jnp.concatenate([vh[h], kh[h]], axis=1), both)
        flat_k[at, :] = dk[h] + result[:, :CHUNK]
        flat_v[at, :] = dv[h] + result[:, CHUNK:]

    work = [masks, functools.partial(inner_grads, 0), functools.partial(inner_grads, 2)]
    work += [functools.partial(diagonal, u) for u in range(9)]

    def do(number=1):
        for _ in range(number):
            if work:
                work.pop(0)()

    do(3)
    found = []
    for n, b in enumerate((3, 2, 1)):
        halves[b].wait_recv()
        after = []
        for s in subs:
            if n:
                now[s].wait_recv()
                value = r_down[n, s] + mid[n - 1, s]
            else:
                pl.when(top == 0)(now[s].wait_recv)
                value = jnp.where(top == 0, r_down[n, s], 0.0)
            mid[n, s] = value
            down[n + 1, s] = value + part(level, s, b) + part(r_level, s, b - 1)
            after.append(remote(down.at[n + 1, s], r_down.at[n + 1, s], b))
            step_up(n + 1, s)
            if SPLIT == 2 or s % 2:
                do()
        now = after
        found.append(remote(r_tot.at[n], r_found.at[n], 0))
    do(len(work))

    def cross_states(p, ref, first):
        value = scale * factor(12 + p)
        is_on = lax.rem(jnp.right_shift(seq, p + 1), 2) == 1
        for s in subs:
            rows = pl.ds(s % SPLIT * half, half)
            cross[p + 1, first + s // SPLIT, rows] = (
                jnp.where(is_on, value * ref[p, s], 0.0)).astype(BF16)

    pl.when(mine != 0)(s_mine.wait_recv)
    for h in range(heads):
        cross[0, h] = jnp.where(mine != 0, scale * factor(11) * r_state[h], 0.0).astype(BF16)
    for p in range(3):
        cross_states(p, r_tot, mine)
        found[p].wait_recv()
        cross_states(p, r_found, theirs)
    for h in range(heads):
        across(h)
    last = []
    pl.when(mine == 0)(whole.wait_recv)
    for s in subs:
        now[s].wait_recv()
        mid[3, s] = mid[2, s] + r_down[3, s]
        last.append(remote(mid.at[3, s], r_mid.at[s], 0))
        rows = pl.ds(s % SPLIT * half, half)
        ks[mine + s // SPLIT, rows] = (
            mid[3, s] + jnp.where(mine == 0, part(r_level0, s), 0.0)).astype(BF16)
        pl.when(top == 1)(up[3][s].wait_recv)
    found.append(remote(r_tot.at[3], r_found.at[3], 0, top == 1))
    cross_states(3, r_tot, mine)
    for i in range(2):
        finish(mine + i)
        across_last(mine + i)
    for s in subs:
        last[s].wait_recv()
        rows = pl.ds(s % SPLIT * half, half)
        ks[theirs + s // SPLIT, rows] = (
            r_mid[s] + jnp.where(mine == 0, r_level0[theirs + s // SPLIT, rows], 0.0)).astype(BF16)
    pl.when(top == 1)(found[3].wait_recv)
    cross_states(3, r_found, theirs)
    for i in range(2):
        finish(theirs + i)
        across_last(theirs + i)
    out_q[...] = tmp[...].astype(BF16)

    rare = dict(some)
    for n, c in enumerate(sent):
        if n in rare:
            pl.when(rare[n])(c.wait_send)
        else:
            c.wait_send()
    for c in codes_sent:
        c.wait_send()


def exchange(scale, zs, heads, q, k, v, g, codes):
    count, width = q.shape[0] // heads, q.shape[1]
    chunks = count // CHUNK
    square = (width, width)
    piece = (4, 2 * SPLIT, CHUNK // SPLIT, width)
    hbm = pl.BlockSpec(memory_space=pltpu.HBM)
    vmem = pl.BlockSpec(memory_space=pltpu.VMEM)
    messages = 2 + 4 + 4 + 1 + 18 * SPLIT
    flat = jax.ShapeDtypeStruct((heads * count, width), F32)
    return pl.pallas_call(
        functools.partial(exchange_kernel, scale, zs),
        out_shape=(jax.ShapeDtypeStruct(flat.shape, BF16), flat, flat),
        in_specs=[hbm] * 5,
        out_specs=(vmem,) * 3,
        scratch_shapes=[
            pltpu.VMEM((4, heads * count, width), BF16),
            pltpu.VMEM((heads * count, width), F32),
            *[pltpu.VMEM((heads, count, width), BF16)] * 4,
            *[pltpu.VMEM((heads, width, count), BF16)] * 3,
            pltpu.VMEM((INNER + CROSS, 16, count), BF16),
            pltpu.VMEM((zs, ROWS, CHUNK), jnp.int32),
            pltpu.VMEM((2, chunks, *square), F32),
            pltpu.VMEM((len(PAIRS), heads, *square), BF16),
            *[pltpu.VMEM((chunks - 1, heads, *square), BF16)] * 2,
            pltpu.VMEM((chunks, CHUNK, CHUNK), F32),
            pltpu.VMEM((2, 4, 2, CHUNK, CHUNK), BF16),
            pltpu.VMEM((heads, width, count), F32),
            *[pltpu.VMEM((heads, count, width), F32)] * 2,
            pltpu.VMEM((CROSS, heads, *square), BF16),
            pltpu.VMEM((heads, *square), BF16),
            pltpu.VMEM((heads, *square), F32),
            pltpu.VMEM((heads, *square), F32),
            *[pltpu.VMEM(piece, F32)] * 3,
            pltpu.VMEM((CROSS, heads, *square), F32),
            pltpu.VMEM((4, heads, *square), F32),
            pltpu.VMEM((heads, *square), F32),
            *[pltpu.VMEM(piece, F32)] * 3,
            pltpu.VMEM(piece[1:], F32),
            pltpu.SemaphoreType.DMA((5,)),
            pltpu.SemaphoreType.DMA((zs - 1,)),
            pltpu.SemaphoreType.DMA((zs - 1,)),
            pltpu.SemaphoreType.DMA((messages,)),
            pltpu.SemaphoreType.DMA((messages,)),
        ],
        compiler_params=pltpu.CompilerParams(
            collective_id=0, has_side_effects=True, vmem_limit_bytes=LIMIT),
        name="exchange",
    )(q, k, v, g, codes)


LIMIT = 44 << 20
PIECES = 4


def pack_kernel(q_in, k_in, v_in, q_out, k_out, v_out, stage, sem):
    rows = q_in.shape[0] // PIECES
    copies = [pltpu.make_async_copy(q_in, q_out, sem.at[2, 0])]
    copies[0].start()
    for n in range(PIECES):
        at = pl.ds(n * rows, rows)
        for i, (src, dst) in enumerate(((k_in, k_out), (v_in, v_out))):
            stage[i, at] = src[at, :].astype(BF16)
            c = pltpu.make_async_copy(stage.at[i, at], dst.at[at], sem.at[i, n])
            c.start()
            copies.append(c)
    for c in copies:
        c.wait()


def pack(*flat):
    shape = flat[0].shape
    return pl.pallas_call(
        pack_kernel,
        out_shape=(jax.ShapeDtypeStruct(shape, BF16),) * 3,
        in_specs=[pl.BlockSpec(memory_space=pltpu.VMEM)] * 3,
        out_specs=(pl.BlockSpec(memory_space=pltpu.HBM),) * 3,
        scratch_shapes=[pltpu.VMEM((2, *shape), BF16), pltpu.SemaphoreType.DMA((3, PIECES))],
        compiler_params=pltpu.CompilerParams(vmem_limit_bytes=16 << 20),
        name="pack",
    )(*flat)


def on_device(queries, keys, values, out_grad, level_codes):
    count, heads, width = queries.shape
    scale = width ** (-0.5)
    flat = [x.reshape(count * heads, width) for x in (queries, keys, values, out_grad)]
    *flat, codes = [
        pltpu.with_memory_space_constraint(x, pltpu.HBM) for x in (*flat, level_codes)]
    grads = pack(*exchange(scale, lax.axis_size("head"), heads, *flat, codes))
    return tuple(x.reshape(count, heads, width) for x in grads)


def solution(mesh):
    return jax.shard_map(
        on_device,
        mesh=mesh,
        in_specs=(
            P("seq", "head", None),
            P("seq", "head", None),
            P("seq", "head", None),
            P("seq", "head", None),
            P(None, ("seq", "head")),
        ),
        out_specs=(P("seq", "head", None), P("seq", "head", None), P("seq", "head", None)),
        check_vma=False,
    )
```
